32 devices in a mesh: groups: 1, leaf: 32 (over z, y, x, core).
Axes of the slice: x: 2, y: 2, z: 4, core: 2. Of those that a mesh axis runs over, the one named last changes fastest.
Arguments:
- embeddings: bfloat16 [768, 65536], P(None, ('groups', 'leaf')), may hold values from -4 to 4
- probes: bfloat16 [32, 65536], P(None, ('groups', 'leaf')), may hold values from -1.75 to 1.75
- order: int32 [32, 2048], P(('groups', 'leaf')), may hold values from 0 to 2047, each once within a row
- near_list: int32 [256, 7], P(('groups', 'leaf')), may hold values from 0 to 255, as said below
- near_count: int32 [32, 8], P(('groups', 'leaf')), may hold values from 1 to 7, 32 in all within a row
- skeleton: int32 [30, 64], P('groups'), may hold values from 0 to 65535, as said below
- core: float32 [30, 64, 64], P('groups'), may hold values from -8 to 8
Outputs:
- values: float32 [32, 65536], P(None, ('groups', 'leaf'))
The draws below stay inside these ranges and needn't reach their ends.
Inputs may be any that keep to these rules, and one draw needn't show every extreme that they name: `near_list`: slot 0 of leaf t holds t; every slot of leaf t holds a leaf within 3 of t. `near_count`: each row sums to 32, and its largest entry is 7. `skeleton`: entry r of node n lies among the examples of node n, in the r-th of 64 equal parts of them. `order`: each row is a permutation.
All inputs are finite; a program needn't handle non-finite values.
Results may differ from the reference program's by a relative error of at most 0.0042.
Values may be sent and summed in bfloat16 or wider, within the bound.
No kernel may reach another device: no remote copies, remote signals or barrier semaphores. Data moves between devices by JAX's collectives and lax.ppermute only.
A program may use at most 128 MiB of HBM per device.

```python
import math
import jax
import jax.numpy as jnp
import numpy as np
from jax import lax

E = 768
P_SIZE = 32
LEAF = 256
R = 64
LEVELS = 4
W = 3
LEAF_DEV = 8
NEAR = 7
PTS_DEV = 2048
PAIRS_DEV = 32
LEAVES = 256
POINTS = 65536
NODES = 30
N_LEAF = 32


def draw_embeddings(key, part):
    harmonic = sum((1.0 / (index_value + 1.0) for index_value in range(E)))
    feature_pos = jnp.arange(E, dtype=jnp.float32)[:, None]
    feature_scale = jnp.sqrt(2.0 / (harmonic * (feature_pos + 1.0)))
    noise = jnp.clip(jax.random.normal(key, (E, POINTS), jnp.float32), -6.0, 6.0)
    return (noise * feature_scale).astype(jnp.bfloat16)


def node_levels(node_ids):
    level_ids = jnp.zeros_like(node_ids)
    for level_id in range(1, LEVELS):
        level_ids = level_ids + (node_ids >= 2 ** (level_id + 1) - 2).astype(jnp.int32)
    return level_ids


def draw_skeleton(key, part):
    node_ids = jnp.arange(NODES, dtype=jnp.int32)[:, None]
    level_ids = node_levels(node_ids)
    level_nodes = jnp.left_shift(jnp.int32(2), level_ids)
    within = node_ids - (level_nodes - 2)
    node_points = POINTS // level_nodes
    stride = node_points // R
    rank_ids = jnp.arange(R, dtype=jnp.int32)[None, :]
    jitter = jax.random.randint(key, (NODES, R), 0, 1 << 30, dtype=jnp.int32) % stride
    return (within * node_points + rank_ids * stride + jitter).astype(jnp.int32)


def draw_core(key, part):
    node_ids = jnp.arange(NODES, dtype=jnp.int32)
    level_ids = node_levels(node_ids)
    node_points = POINTS / jnp.exp2(level_ids.astype(jnp.float32) + 1.0)
    spread = 15.0 / jnp.sqrt(R * node_points)
    noise = jnp.clip(jax.random.normal(key, (NODES, R, R), jnp.float32), -6.0, 6.0)
    return noise * spread[:, None, None]


def draw_near_list(key, part):
    leaf_ids = jnp.arange(LEAVES, dtype=jnp.int32)[:, None]
    steps_pool = jnp.concatenate([jnp.arange(-W, 0, dtype=jnp.int32), jnp.arange(1, W + 1, dtype=jnp.int32)])
    scores = jax.random.randint(key, (LEAVES, 2 * W), 0, 1 << 20, dtype=jnp.int32) * (2 * W) + jnp.arange(2 * W, dtype=jnp.int32)[None, :]
    ranking = jnp.argsort(scores, axis=1, stable=True)
    offsets = steps_pool[ranking]
    neighbours = leaf_ids + offsets
    mirrored = leaf_ids - offsets
    neighbours = jnp.where((neighbours < 0) | (neighbours >= LEAVES), mirrored, neighbours)
    return jnp.concatenate([leaf_ids, neighbours], axis=1).astype(jnp.int32)


def steps_of(rng, dims, cuts, low, largest):
    loudness = 1.0
    for axis_at, blocks in cuts:
        heights = jax.random.uniform(jax.random.fold_in(jax.random.fold_in(rng, 6), axis_at), (blocks,), jnp.float32, low / len(cuts), largest / len(cuts))
        loudness = loudness * jnp.repeat(jnp.exp(heights), dims[axis_at] // blocks).reshape((-1,) + (1,) * (len(dims) - 1 - axis_at))
    return loudness


def split_up(count, total, bound, skew):
    weights = [(1 << 20) // math.isqrt(grade ** skew) + 1 for grade in range(2, count + 1)]
    surplus, counts = total - bound - (count - 1), [1] * (count - 1)
    while surplus > 0:
        candidates = [i for i in range(count - 1) if counts[i] < bound]
        whole, left = sum([weights[i] for i in candidates]), surplus
        for i in candidates:
            extra = min(bound - counts[i], max(1, left * weights[i] // whole), surplus)
            counts[i] = counts[i] + extra
            surplus = surplus - extra
    return np.array([bound] + counts)


def uneven_parts(rng, amount, total, reach, lean):
    if amount == 2:
        one = jax.random.randint(rng, (), max(1, total - reach), min(reach, total - 1) + 1)
        return jnp.stack([one, total - one])
    lengths = jnp.asarray(split_up(amount, total, reach, lean), jnp.int32)
    couples = (amount - 1) // 2
    source_of, taker = lengths[1:1 + 2 * couples:2], lengths[2:2 + 2 * couples:2]
    margin = jnp.minimum(source_of - 1, reach - taker)
    shifted = jax.random.randint(jax.random.fold_in(rng, 1), (couples,), 0, 1 << 20) % (margin + 1)
    lengths = lengths.at[1:1 + 2 * couples:2].set(source_of - shifted).at[2:2 + 2 * couples:2].set(taker + shifted)
    return lengths[jax.random.permutation(jax.random.fold_in(rng, 2), amount)]


def centred(key, extent, scale, limit, cuts=(), held_as=jnp.bfloat16):
    result = jax.random.normal(key, extent, jnp.float32) * scale
    if len(cuts) > 0:
        result = steps_of(key, extent, cuts, -0.22, 0.18) * result
    return jnp.clip(result, min=-limit, max=limit).astype(held_as)


def setup_inputs(seed: int = 0, part: int = 0) -> dict:
    splits = jax.random.split(jax.random.key(seed), 8)
    part_splits = jax.random.split(jax.random.fold_in(splits[7], part), 8)
    return {
        "embeddings": draw_embeddings(jax.random.fold_in(jax.random.fold_in(splits[7], part), 71), part),
        "probes": centred(part_splits[1], (P_SIZE, POINTS), 0.3, 1.75, ((1, 32),)),
        "order": jax.vmap(lambda own: jax.random.permutation(own, PTS_DEV))(jax.random.split(part_splits[2], N_LEAF)).reshape((N_LEAF, PTS_DEV)).astype(jnp.int32),
        "near_list": draw_near_list(jax.random.fold_in(jax.random.fold_in(splits[7], part), 71), part),
        "near_count": jax.vmap(lambda own: uneven_parts(own, LEAF_DEV, PAIRS_DEV, NEAR, 1))(jax.random.split(part_splits[4], N_LEAF)).reshape((N_LEAF, LEAF_DEV)).astype(jnp.int32),
        "skeleton": draw_skeleton(jax.random.fold_in(jax.random.fold_in(splits[7], part), 71), part),
        "core": draw_core(jax.random.fold_in(jax.random.fold_in(splits[7], part), 71), part),
    }


def kernel_matrix(left_emb, left_norm, right_emb, right_norm):
    inner = lax.dot_general(left_emb, right_emb, (((0,), (0,)), ((), ())), preferred_element_type=jnp.float32)
    distance = left_norm[:, None] + right_norm[None, :] - 2.0 * inner
    return jnp.exp(-0.5 * distance).astype(jnp.bfloat16)


def reference(embeddings, probes, order, near_list, near_count, skeleton, core):
    offsets_dev = (jnp.arange(N_LEAF, dtype=jnp.int32) * PTS_DEV)[:, None]
    tree_index = (order + offsets_dev).reshape(-1).astype(jnp.int32)
    x_tree = probes[:, tree_index]
    norms = jnp.sum(jnp.square(embeddings.astype(jnp.float32)), axis=0)
    emb_leaf = embeddings.reshape(E, LEAVES, LEAF)
    norm_leaf = norms.reshape(LEAVES, LEAF)
    x_leaf = x_tree.reshape(P_SIZE, LEAVES, LEAF)
    live = (jnp.arange(NEAR, dtype=jnp.int32)[None, :] < near_count.reshape(-1)[:, None]).reshape(-1)
    flat_ids = jnp.nonzero(live, size=N_LEAF * PAIRS_DEV)[0].astype(jnp.int32)
    targets = (flat_ids // NEAR).astype(jnp.int32)
    sources = near_list.reshape(-1)[flat_ids].astype(jnp.int32)

    def pair_term(pair):
        target, source = pair
        kernel_vals = kernel_matrix(emb_leaf[:, source], norm_leaf[source], emb_leaf[:, target], norm_leaf[target])
        return jnp.dot(x_leaf[:, source], kernel_vals, preferred_element_type=jnp.float32)

    terms = lax.map(pair_term, (targets, sources))
    near_sum = jax.ops.segment_sum(terms, targets, num_segments=LEAVES)
    near_sum = jnp.transpose(near_sum, (1, 0, 2)).reshape(P_SIZE, POINTS)

    far_sum = jnp.zeros((P_SIZE, POINTS), jnp.float32)
    for level_id in range(LEVELS):
        node_total = 2 ** (level_id + 1)
        first_node = node_total - 2
        node_points = POINTS // node_total
        level_skel = skeleton[first_node:first_node + node_total].reshape(-1)
        skel_emb = embeddings[:, level_skel].reshape(E, node_total, R)
        skel_norm = norms[level_skel].reshape(node_total, R)
        blocks_emb = embeddings.reshape(E, node_total, node_points)
        blocks_norm = norms.reshape(node_total, node_points)
        blocks_x = x_tree.reshape(P_SIZE, node_total, node_points)
        level_core = core[first_node:first_node + node_total]

        def node_sum(node_id):
            kernel_vals = kernel_matrix(blocks_emb[:, node_id], blocks_norm[node_id], skel_emb[:, node_id], skel_norm[node_id])
            return jnp.dot(blocks_x[:, node_id], kernel_vals, preferred_element_type=jnp.float32)

        node_ids = jnp.arange(node_total, dtype=jnp.int32)
        sums = lax.map(node_sum, node_ids)
        weights = jnp.einsum("npr,nrs->nps", sums, level_core, precision=lax.Precision.HIGHEST).astype(jnp.bfloat16)

        def node_apply(node_id):
            partner = jnp.bitwise_xor(node_id, 1)
            kernel_vals = kernel_matrix(skel_emb[:, partner], skel_norm[partner], blocks_emb[:, node_id], blocks_norm[node_id])
            return jnp.dot(weights[partner], kernel_vals, preferred_element_type=jnp.float32)

        applied = lax.map(node_apply, node_ids)
        far_sum = far_sum + jnp.transpose(applied, (1, 0, 2)).reshape(P_SIZE, POINTS)

    tree_values = near_sum + far_sum
    return jnp.zeros((P_SIZE, POINTS), jnp.float32).at[:, tree_index].set(tree_values)
```

```python
import jax
import jax.numpy as jnp
from jax import lax
from jax.experimental import pallas as pl
from jax.experimental.pallas import tpu as pltpu
from jax.sharding import PartitionSpec as P

LEAF = 256
R = 64
LEVELS = 4
W = 3
F32 = jnp.float32
BF16 = jnp.bfloat16
VMEM_LIMIT = 48 * 1024 * 1024


def dot(a, b):
    return jnp.dot(a, b, preferred_element_type=F32)


def dot_nt(a, b):
    return lax.dot_general(a, b, (((1,), (1,)), ((), ())), preferred_element_type=F32)


def dot_tn(a, b):
    return lax.dot_general(a, b, (((0,), (0,)), ((), ())), preferred_element_type=F32)


def half_norm_row(emb):
    e = emb.astype(F32)
    return 0.5 * jnp.sum(e * e, axis=0, keepdims=True)


def half_norm_col(rows):
    e = rows.astype(F32)
    return 0.5 * jnp.sum(e * e, axis=1, keepdims=True)


def call(kernel, outs, *args, scratch=(), smem=(), flops=0, nbytes=0, name=None):
    single = not isinstance(outs, (list, tuple))
    vm = pl.BlockSpec(memory_space=pltpu.VMEM)
    sm = pl.BlockSpec(memory_space=pltpu.SMEM)
    res = pl.pallas_call(
        kernel,
        out_shape=outs,
        in_specs=[sm if i in smem else vm for i in range(len(args))],
        out_specs=vm if single else [vm] * len(outs),
        scratch_shapes=list(scratch),
        compiler_params=pltpu.CompilerParams(vmem_limit_bytes=VMEM_LIMIT),
        cost_estimate=pl.CostEstimate(flops=flops, bytes_accessed=nbytes, transcendentals=0),
        name=name,
    )(*args)
    return res


class Plan:
    def __init__(self, n):
        self.n = n
        self.bits = n.bit_length() - 1
        self.slots = [R * 2 ** (l + 1) // n for l in range(LEVELS)]
        self.padded = [-(-s // 8) * 8 for s in self.slots]
        self.starts = [sum(self.padded[:l]) for l in range(LEVELS)]
        self.rows = sum(self.padded)
        self.shift = [self.bits - 1 - l for l in range(LEVELS)]
        entries, size = [], 0
        for bit in reversed(range(self.bits)):
            level = self.bits - 1 - bit
            if level < LEVELS:
                entries.append((level, 0, size))
                size += self.padded[level]
            entries += [(lev, off ^ (1 << bit), row + size) for lev, off, row in entries]
            size *= 2
        self.entries, self.size = entries, size


def body(embeddings, probes, order, near_list, near_count, skeleton, core):
    n = lax.axis_size("leaf")
    plan = Plan(n)
    pos = lax.axis_index("leaf")
    width, points = embeddings.shape
    cols = probes.shape[0]
    leaves = points // LEAF
    halo = W * LEAF

    def pick_kernel(skel_ref, emb_ref, g_ref, row_ref):
        me = lax.axis_index("leaf")
        lane = lax.broadcasted_iota(jnp.int32, (1, 128), 1)
        idx = jnp.full((1, 128), -1, jnp.int32)
        row_ref[...] = jnp.zeros_like(row_ref)
        for l in range(LEVELS):
            node = 2 ** (l + 1) - 2 + jnp.right_shift(me, plan.shift[l])
            row_ref[0:1, 0:R] = skel_ref[pl.ds(node, 1), :]
            within = jnp.bitwise_and(me, (1 << plan.shift[l]) - 1)
            shift = jnp.bitwise_and(plan.starts[l] - within * plan.slots[l] + 128, 127)
            rolled = pltpu.roll(row_ref[...], shift, 1)[0:1, :]
            mine = (lane >= plan.starts[l]) & (lane < plan.starts[l] + plan.slots[l])
            idx = jnp.where(mine, rolled - me * points, idx)
        acc = jnp.zeros((width, 128), F32)
        for c in range(points // LEAF):
            at = lax.broadcasted_iota(jnp.int32, (LEAF, 128), 0) + c * LEAF
            hot = jnp.where(at == idx, 1.0, 0.0).astype(BF16)
            acc = acc + dot(emb_ref[:, c * LEAF : (c + 1) * LEAF], hot)
        g_ref[...] = jnp.transpose(acc)[: plan.rows].astype(BF16)

    owned = call(
        pick_kernel,
        jax.ShapeDtypeStruct((plan.rows, width), BF16),
        skeleton,
        embeddings,
        scratch=[pltpu.VMEM((8, 128), jnp.int32)],
        name="pick",
    )

    def tree_kernel(order_ref, probes_ref, emb_ref, x_ref, inv_ref, a_ref, b_ref):
        me = lax.axis_index("leaf")
        inv = jnp.zeros((8, points), F32)
        sub = lax.broadcasted_iota(jnp.int32, (8, LEAF), 0)
        at = lax.broadcasted_iota(jnp.int32, (points, LEAF), 0)
        for c in range(leaves):
            sl = slice(c * LEAF, (c + 1) * LEAF)
            hot = jnp.where(at == order_ref[0:1, sl], 1.0, 0.0).astype(BF16)
            x_ref[:, sl] = dot(probes_ref[...], hot).astype(BF16)
            k = lax.broadcasted_iota(jnp.int32, (8, LEAF), 1) + c * LEAF
            parts = jnp.where(sub == 0, jnp.right_shift(k, 4), jnp.bitwise_and(k, 15))
            inv = inv + dot_nt(parts.astype(F32).astype(BF16), hot)
        inv_ref[...] = (inv[0:1] * 16.0 + inv[1:2]).astype(jnp.int32)
        first, last = slice(0, halo), slice(points - halo, points)

        def put(ref, sl):
            ref[0:width, :] = emb_ref[:, sl]
            ref[width : width + cols, :] = x_ref[:, sl]

        odd = jnp.bitwise_and(me, 1)

        @pl.when(odd == 0)
        def _():
            put(a_ref, last)
            put(b_ref, first)

        @pl.when(odd == 1)
        def _():
            put(a_ref, first)
            put(b_ref, last)

    send = jax.ShapeDtypeStruct((width + cols, halo), BF16)
    x_tree, inv, send_a, send_b = call(
        tree_kernel,
        [
            jax.ShapeDtypeStruct((cols, points), BF16),
            jax.ShapeDtypeStruct((1, points), jnp.int32),
            send,
            send,
        ],
        order,
        probes,
        embeddings,
        name="tree",
    )
    pairs_a = [(i, i ^ 1) for i in range(n)]
    pairs_b = [(i, i + 1) for i in range(1, n - 1, 2)] + [(i + 1, i) for i in range(1, n - 1, 2)]
    recv_a = lax.ppermute(send_a, "leaf", pairs_a)
    recv_b = lax.ppermute(send_b, "leaf", pairs_b)

    reach = jnp.arange(-W, W + 1, dtype=jnp.int32)
    target = pos * leaves + jnp.arange(leaves, dtype=jnp.int32)
    live = jnp.arange(near_list.shape[1], dtype=jnp.int32)[None, :] < near_count[0][:, None]
    same = near_list[:, :, None] == target[:, None, None] + reach[None, None, :]
    mult = jnp.sum(jnp.where(same & live[:, :, None], 1.0, 0.0), axis=1).astype(F32)

    def near_kernel(rows, mult_ref, emb_ref, x_ref, near_ref):
        near_ref[...] = jnp.zeros_like(near_ref)
        hn = half_norm_row(emb_ref[...])
        for i in rows:
            si = slice(i * LEAF, (i + 1) * LEAF)
            ei = jnp.transpose(emb_ref[:, si])
            hi = half_norm_col(ei)
            for j in range(i, min(i + W + 1, leaves)):
                sj = slice(j * LEAF, (j + 1) * LEAF)
                k = jnp.exp(dot(ei, emb_ref[:, sj]) - (hi + hn[:, sj])).astype(BF16)
                near_ref[:, sj] += mult_ref[j, i - j + W] * dot(x_ref[:, si], k)
                if j > i:
                    near_ref[:, si] += mult_ref[i, j - i + W] * dot_nt(x_ref[:, sj], k)

    parts = []
    for rows in ((0, 1), (2, 3), (4, 5, 6, 7)):
        parts.append(
            call(
                lambda *refs, rows=rows: near_kernel(rows, *refs),
                jax.ShapeDtypeStruct((cols, points), F32),
                mult,
                embeddings,
                x_tree,
                smem=(0,),
                flops=10 * 5 * 2 * 256**3,
                nbytes=6 << 20,
                name="near%d" % rows[0],
            )
        )

    block = None
    for bit in reversed(range(plan.bits)):
        level = plan.bits - 1 - bit
        if level < LEVELS:
            own = lax.slice_in_dim(
                owned, plan.starts[level], plan.starts[level] + plan.padded[level], axis=0
            )
            block = own if block is None else jnp.concatenate([block, own], axis=0)
        other = lax.ppermute(block, "leaf", [(i, i ^ (1 << bit)) for i in range(n)])
        block = jnp.concatenate([block, other], axis=0)

    offs, base, mask, slot, ok = [], [], [], [], []
    side = []
    for lev, off, row in sorted(plan.entries, key=lambda e: e[2]):
        for i in range(plan.padded[lev]):
            offs.append(off)
            side.append((off >> plan.shift[lev]) & 1)
            base.append(lev * R + i)
            mask.append((1 << plan.shift[lev]) - 1)
            slot.append(plan.slots[lev])
            ok.append(1 if i < plan.slots[lev] else 0)
    table = jnp.array([offs, side, base, mask, slot, ok], jnp.int32)
    own_w = LEVELS * R
    dest = table[1] * own_w + table[2] + jnp.bitwise_and(pos ^ table[0], table[3]) * table[4]
    dest = jnp.where(table[5] == 1, dest, -1)[None, :]

    def own_kernel(block_ref, dest_ref, emb_ref, x_ref, z_ref, part_ref):
        at = lax.broadcasted_iota(jnp.int32, (2 * own_w, plan.size), 0)
        hot = jnp.where(at == dest_ref[...], 1.0, 0.0).astype(BF16)
        sk = dot(hot, block_ref[...]).astype(BF16)
        part_ref[...] = sk[own_w:]
        hs = half_norm_col(sk[:own_w])
        z = jnp.zeros((cols, own_w), F32)
        for c in range(leaves):
            sl = slice(c * LEAF, (c + 1) * LEAF)
            e = emb_ref[:, sl]
            k = jnp.exp(dot(sk[:own_w], e) - (hs + half_norm_row(e))).astype(BF16)
            z = z + dot_nt(x_ref[:, sl], k)
        z_ref[...] = z

    z, part = call(
        own_kernel,
        [jax.ShapeDtypeStruct((cols, own_w), F32), jax.ShapeDtypeStruct((own_w, width), BF16)],
        block,
        dest,
        embeddings,
        x_tree,
        flops=30 * 2 * 256**3,
        nbytes=4 << 20,
        name="own",
    )

    level_of = lax.broadcasted_iota(jnp.int32, (1, own_w), 1) // R
    for bit in range(plan.bits):
        other = lax.ppermute(z, "leaf", [(i, i ^ (1 << bit)) for i in range(n)])
        swap = level_of == plan.bits - 1 - bit
        add = level_of < plan.bits - 1 - bit
        z = jnp.where(add, z + other, jnp.where(swap, other, z))

    def far_kernel(part_ref, emb_ref, inv_ref, out_ref, k_ref):
        hs = half_norm_col(part_ref[...])
        for c in range(leaves):
            sl = slice(c * LEAF, (c + 1) * LEAF)
            e = emb_ref[:, sl]
            k_ref[:, sl] = jnp.exp(dot(part_ref[...], e) - (hs + half_norm_row(e))).astype(BF16)
        at = lax.broadcasted_iota(jnp.int32, (points, LEAF), 0)
        for c in range(leaves):
            sl = slice(c * LEAF, (c + 1) * LEAF)
            hot = jnp.where(at == inv_ref[0:1, sl], 1.0, 0.0).astype(BF16)
            out_ref[:, sl] = dot(k_ref[...], hot).astype(BF16)

    far_k = call(
        far_kernel,
        jax.ShapeDtypeStruct((own_w, points), BF16),
        part,
        embeddings,
        inv,
        scratch=[pltpu.VMEM((own_w, points), BF16)],
        flops=90 * 2 * 256**3,
        nbytes=4 << 20,
        name="far",
    )

    def edge_kernel(mult_ref, emb_ref, x_ref, a_ref, b_ref, inv_ref, *rest):
        part_refs, (out_ref, near_ref) = rest[:-2], rest[-2:]
        near = part_refs[0][...]
        for ref in part_refs[1:]:
            near = near + ref[...]
        near_ref[...] = near
        odd = jnp.bitwise_and(lax.axis_index("leaf"), 1)

        def edges(low_ref, high_ref):
            for t in range(W):
                st = slice(t * LEAF, (t + 1) * LEAF)
                et = emb_ref[:, st]
                ht = half_norm_row(et)
                for q in range(t, W):
                    sq = slice(q * LEAF, (q + 1) * LEAF)
                    es = jnp.transpose(low_ref[0:width, sq])
                    k = jnp.exp(dot(es, et) - (half_norm_col(es) + ht)).astype(BF16)
                    near_ref[:, st] += mult_ref[t, q - t] * dot(
                        low_ref[width : width + cols, sq], k
                    )
            for back in range(W):
                t = leaves - 1 - back
                st = slice(t * LEAF, (t + 1) * LEAF)
                et = emb_ref[:, st]
                ht = half_norm_row(et)
                for q in range(W - back):
                    sq = slice(q * LEAF, (q + 1) * LEAF)
                    es = jnp.transpose(high_ref[0:width, sq])
                    k = jnp.exp(dot(es, et) - (half_norm_col(es) + ht)).astype(BF16)
                    near_ref[:, st] += mult_ref[t, back + 1 + q + W] * dot(
                        high_ref[width : width + cols, sq], k
                    )

        @pl.when(odd == 1)
        def _():
            edges(a_ref, b_ref)

        @pl.when(odd == 0)
        def _():
            edges(b_ref, a_ref)

        full = near_ref[...]
        high = full.astype(BF16)
        rest_1 = full - high.astype(F32)
        mid = rest_1.astype(BF16)
        low = (rest_1 - mid.astype(F32)).astype(BF16)
        both = jnp.concatenate([high, mid, low], axis=0)
        at = lax.broadcasted_iota(jnp.int32, (points, LEAF), 0)
        for c in range(leaves):
            sl = slice(c * LEAF, (c + 1) * LEAF)
            hot = jnp.where(at == inv_ref[0:1, sl], 1.0, 0.0).astype(BF16)
            res = dot(both, hot)
            out_ref[:, sl] = res[:cols] + res[cols : 2 * cols] + res[2 * cols :]

    near = call(
        edge_kernel,
        jax.ShapeDtypeStruct((cols, points), F32),
        mult,
        embeddings,
        x_tree,
        recv_a,
        recv_b,
        inv,
        *parts,
        scratch=[pltpu.VMEM((cols, points), F32)],
        smem=(0,),
        flops=70 * 2 * 256**3,
        nbytes=6 << 20,
        name="edge",
    )

    def last_kernel(z_ref, core_ref, far_ref, near_ref, out_ref):
        me = lax.axis_index("leaf")
        weights = []
        for l in range(LEVELS):
            node = 2 ** (l + 1) - 2 + (jnp.right_shift(me, plan.shift[l]) ^ 1)
            weights.append(
                jnp.dot(
                    z_ref[:, l * R : (l + 1) * R],
                    core_ref[node],
                    precision=lax.Precision.HIGHEST,
                    preferred_element_type=F32,
                ).astype(BF16)
            )
        w = jnp.concatenate(weights, axis=1)
        for c in range(leaves):
            sl = slice(c * LEAF, (c + 1) * LEAF)
            out_ref[:, sl] = near_ref[:, sl] + dot(w, far_ref[:, sl])

    return call(
        last_kernel,
        jax.ShapeDtypeStruct((cols, points), F32),
        z,
        core,
        far_k,
        near,
        flops=8 * 2 * 256**3,
        nbytes=2 << 20,
        name="last",
    )


def solution(mesh):
    return jax.shard_map(
        body,
        mesh=mesh,
        in_specs=(
            P(None, ("groups", "leaf")),
            P(None, ("groups", "leaf")),
            P(("groups", "leaf"), None),
            P(("groups", "leaf"), None),
            P(("groups", "leaf"), None),
            P("groups", None),
            P("groups", None, None),
        ),
        out_specs=P(None, ("groups", "leaf")),
        check_vma=False,
    )
```

```python
import jax
import jax.numpy as jnp
from jax import lax
from jax.experimental import pallas as pl
from jax.experimental.pallas import tpu as pltpu
from jax.sharding import PartitionSpec as P

LEAF = 256
R = 64
LEVELS = 4
W = 3
F32 = jnp.float32
BF16 = jnp.bfloat16
VMEM_LIMIT = 14 * 1024 * 1024
LANES = 128
UP, DOWN = 2, 1


def dot(a, b):
    return jnp.dot(a, b, preferred_element_type=F32)


def dot_nt(a, b):
    return lax.dot_general(a, b, (((1,), (1,)), ((), ())), preferred_element_type=F32)


def dot_tn(a, b):
    return lax.dot_general(a, b, (((0,), (0,)), ((), ())), preferred_element_type=F32)


def half_norm_row(emb):
    e = emb.astype(F32)
    return 0.5 * jnp.sum(e * e, axis=0, keepdims=True)


def half_norm_col(rows):
    e = rows.astype(F32)
    return 0.5 * jnp.sum(e * e, axis=1, keepdims=True)


def col_of(row):
    return jnp.transpose(jnp.broadcast_to(row, (8, row.shape[1])))[:, 0:1]


def call(kernel, outs, *args, scratch=(), smem=(), hbm=(), flops=0, nbytes=0, name=None, vmem=VMEM_LIMIT):
    single = not isinstance(outs, (list, tuple))
    vm = pl.BlockSpec(memory_space=pltpu.VMEM)
    sm = pl.BlockSpec(memory_space=pltpu.SMEM)
    hb = pl.BlockSpec(memory_space=pltpu.HBM)
    return pl.pallas_call(
        kernel,
        out_shape=outs,
        in_specs=[sm if i in smem else hb if i in hbm else vm for i in range(len(args))],
        out_specs=vm if single else [vm] * len(outs),
        scratch_shapes=list(scratch),
        compiler_params=pltpu.CompilerParams(vmem_limit_bytes=vmem),
        cost_estimate=pl.CostEstimate(flops=flops, bytes_accessed=nbytes, transcendentals=0),
        name=name,
    )(*args)


class Plan:
    def __init__(self, n):
        self.n = n
        self.bits = n.bit_length() - 1
        self.slots = [R * 2 ** (l + 1) // n for l in range(LEVELS)]
        self.padded = [-(-s // 8) * 8 for s in self.slots]
        self.starts = [sum(self.padded[:l]) for l in range(LEVELS)]
        self.rows = sum(self.padded)
        self.shift = [self.bits - 1 - l for l in range(LEVELS)]
        entries, size = [], 0
        for bit in reversed(range(self.bits)):
            level = self.bits - 1 - bit
            if level < LEVELS:
                entries.append((level, 0, size))
                size += self.padded[level]
            entries += [(lev, off ^ (1 << bit), row + size) for lev, off, row in entries]
            size *= 2
        self.entries, self.size = entries, size


def body(embeddings, probes, order, near_list, near_count, skeleton, core):
    n = lax.axis_size("leaf")
    plan = Plan(n)
    pos = lax.axis_index("leaf")
    width, points = embeddings.shape
    cols = probes.shape[0]
    leaves = points // LEAF
    halo = W * LEAF

    groups = points // LANES

    last = points - halo
    extra = 16

    def pick_kernel(skel_ref, emb_ref, *rest):
        g_refs, row_ref = rest[:-1], rest[-1]
        me = lax.axis_index("leaf")
        lane = lax.broadcasted_iota(jnp.int32, (1, LANES), 1)
        idx = jnp.full((1, LANES), -1, jnp.int32)
        row_ref[...] = jnp.zeros_like(row_ref)
        for l in range(LEVELS):
            node = 2 ** (l + 1) - 2 + jnp.right_shift(me, plan.shift[l])
            row_ref[0:1, 0:R] = skel_ref[pl.ds(node, 1), :]
            within = jnp.bitwise_and(me, (1 << plan.shift[l]) - 1)
            shift = jnp.bitwise_and(plan.starts[l] - within * plan.slots[l] + LANES, LANES - 1)
            rolled = pltpu.roll(row_ref[...], shift, 1)[0:1, :]
            mine = (lane >= plan.starts[l]) & (lane < plan.starts[l] + plan.slots[l])
            idx = jnp.where(mine, rolled, idx)
        acc = jnp.zeros((width, LANES), F32)
        for c in range(leaves):
            at = lax.broadcasted_iota(jnp.int32, (LEAF, LANES), 0) + c * LEAF
            pick = jnp.where(at == idx, 1.0, 0.0).astype(BF16)
            acc = acc + dot(emb_ref[:, c * LEAF : (c + 1) * LEAF], pick)
        picked = jnp.transpose(acc)
        for l in range(LEVELS):
            g_refs[l][...] = picked[plan.starts[l] : plan.starts[l] + plan.padded[l]].astype(BF16)

    owned = call(
        pick_kernel,
        [jax.ShapeDtypeStruct((p, width), BF16) for p in plan.padded],
        skeleton - pos * points,
        embeddings,
        scratch=[pltpu.VMEM((8, LANES), jnp.int32)],
        flops=10 * 2 * 256**3,
        nbytes=6 << 20,
        name="pick",
    )

    def cut_kernel(emb_ref, up_ref, down_ref, a_ref, sems):
        odd = jnp.bitwise_and(lax.axis_index("leaf"), 1)
        copies = []
        for i, (ref, at) in enumerate(
            ((up_ref, points - UP * LEAF), (down_ref, 0), (a_ref, (1 - odd) * last))
        ):
            at = pl.multiple_of(at, LEAF)
            copies.append(
                pltpu.make_async_copy(emb_ref.at[:, pl.ds(at, ref.shape[1])], ref, sems.at[i])
            )
        for copy in copies:
            copy.start()
        for copy in copies:
            copy.wait()

    emb = embeddings
    send_up, send_down, send_a = call(
        cut_kernel,
        [jax.ShapeDtypeStruct((width, w * LEAF), BF16) for w in (UP, DOWN, W)],
        emb,
        scratch=[pltpu.SemaphoreType.DMA((3,))],
        nbytes=3 << 20,
        name="cut",
    )

    reach = jnp.arange(-W, W + 1, dtype=jnp.int32)
    target = pos * leaves + jnp.arange(leaves, dtype=jnp.int32)
    live = jnp.arange(near_list.shape[1], dtype=jnp.int32)[None, :] < near_count[0][:, None]
    same = near_list[:, :, None] == target[:, None, None] + reach[None, None, :]
    mult = jnp.sum(jnp.where(same & live[:, :, None], 1.0, 0.0), axis=1).astype(F32)

    def tree_kernel(order_ref, probes_ref, emb_ref, mult_ref, x_ref, inv_ref, hn_ref, a_ref, b_ref):
        odd = jnp.bitwise_and(lax.axis_index("leaf"), 1)

        order_row = order_ref[...]
        low = jnp.bitwise_and(order_row, LANES - 1)
        high = jnp.right_shift(order_row, LANES.bit_length() - 1)
        hot = jnp.where(
            lax.broadcasted_iota(jnp.int32, (LANES, points), 0) == low, 1.0, 0.0
        ).astype(BF16)
        stack = jnp.concatenate(
            [probes_ref[:, h * LANES : (h + 1) * LANES] for h in range(groups)], axis=0
        )
        for c in range(leaves):
            sl = slice(c * LEAF, (c + 1) * LEAF)
            y = dot(stack, hot[:, sl])
            x = jnp.zeros((cols, LEAF), F32)
            for h in range(groups):
                x = x + jnp.where(high[:, sl] == h, y[h * cols : (h + 1) * cols], 0.0)
            x_ref[:, sl] = x.astype(BF16)
            hn_ref[:, sl] = half_norm_row(emb_ref[:, sl])

        k = lax.broadcasted_iota(jnp.int32, (8, points), 1)
        sub = lax.broadcasted_iota(jnp.int32, (8, points), 0)
        digits = jnp.where(sub == 0, jnp.right_shift(k, 4), jnp.bitwise_and(k, 15)).astype(F32)
        spread = jnp.concatenate(
            [jnp.where(high == h, digits, 0.0) for h in range(groups)], axis=0
        ).astype(BF16)
        found = dot_nt(spread, hot)
        for h in range(groups):
            inv_ref[:, h * LANES : (h + 1) * LANES] = (
                found[8 * h : 8 * h + 1] * 16.0 + found[8 * h + 1 : 8 * h + 2]
            ).astype(jnp.int32)

        def tell(pairs):
            rows = [jnp.full((1, halo), mult_ref[t, o + W], F32) for t, o in pairs]
            rows.append(jnp.zeros((extra - len(rows), halo), F32))
            b_ref[cols:, :] = jnp.concatenate(rows, axis=0).astype(BF16)

        @pl.when(odd == 0)
        def _():
            a_ref[...] = x_ref[:, last:]
            b_ref[0:cols, :] = x_ref[:, :halo]
            tell([(0, -1 - q) for q in range(W)])

        @pl.when(odd == 1)
        def _():
            a_ref[...] = x_ref[:, :halo]
            b_ref[0:cols, :] = x_ref[:, last:]
            tell([(leaves - 1, 2), (leaves - 1, 3), (leaves - 2, 3)])

    x_send = jax.ShapeDtypeStruct((cols, halo), BF16)
    x_tree, inv, hn, x_a, x_b = call(
        tree_kernel,
        [
            jax.ShapeDtypeStruct((cols, points), BF16),
            jax.ShapeDtypeStruct((1, points), jnp.int32),
            jax.ShapeDtypeStruct((1, points), F32),
            x_send,
            jax.ShapeDtypeStruct((cols + extra, halo), BF16),
        ],
        order,
        probes,
        emb,
        mult,
        smem=(3,),
        flops=40 * 2 * 256**3,
        nbytes=1 << 20,
        name="tree",
    )

    pairs_a = [(i, i ^ 1) for i in range(n)]
    pairs_up = [(i, i + 1) for i in range(1, n - 1, 2)]
    pairs_down = [(j, i) for i, j in pairs_up]

    def near_kernel(rows, mult_ref, emb_ref, x_ref, hn_ref, near_ref):
        acc = [None] * leaves

        def add(j, value):
            acc[j] = value if acc[j] is None else acc[j] + value

        def make(i):
            w = min(W + 1, leaves - i)
            si, sp = slice(i * LEAF, (i + 1) * LEAF), slice(i * LEAF, (i + w) * LEAF)
            g = dot(jnp.transpose(emb_ref[:, si]), emb_ref[:, sp])
            return jnp.exp(g - (col_of(hn_ref[:, si]) + hn_ref[:, sp])).astype(BF16)

        def use(i, k):
            y = dot(x_ref[:, i * LEAF : (i + 1) * LEAF], k)
            for q in range(k.shape[1] // LEAF):
                j = i + q
                sq = slice(q * LEAF, (q + 1) * LEAF)
                add(j, mult_ref[j, W - q] * y[:, sq])
                if q:
                    sj = slice(j * LEAF, (j + 1) * LEAF)
                    add(i, mult_ref[i, W + q] * dot_nt(x_ref[:, sj], k[:, sq]))

        held = None
        for i in rows:
            k = make(i)
            if held is not None:
                use(*held)
            held = (i, k)
        use(*held)
        for j in range(leaves):
            sj = slice(j * LEAF, (j + 1) * LEAF)
            near_ref[:, sj] = jnp.zeros((cols, LEAF), F32) if acc[j] is None else acc[j]

    def near_part(rows, emb, x_tree, hn):
        return call(
            lambda *refs: near_kernel(rows, *refs),
            jax.ShapeDtypeStruct((cols, points), F32),
            mult,
            emb,
            x_tree,
            hn,
            smem=(0,),
            flops=60 * 2 * 256**3,
            nbytes=6 << 20,
            name="near%d" % rows[0],
        )

    def join_kernel(*refs):
        row = 0
        for ref in refs[:-1]:
            refs[-1][row : row + ref.shape[0], :] = ref[...]
            row += ref.shape[0]

    def join(*blocks):
        rows = sum(v.shape[0] for v in blocks)
        return call(
            join_kernel, jax.ShapeDtypeStruct((rows, width), BF16), *blocks, nbytes=1 << 18, name="join"
        )

    after = lax.optimization_barrier
    parts = []
    block = owned[0]
    for bit in reversed(range(plan.bits)):
        level = plan.bits - bit
        stage = level - 1
        partner = lax.ppermute(block, "leaf", [(i, i ^ (1 << bit)) for i in range(n)])
        if stage == 0:
            recv_up = lax.ppermute(send_up, "leaf", pairs_up)
            recv_down = lax.ppermute(send_down, "leaf", pairs_down)
            partner, x_tree = after((partner, x_tree))
        if stage == 1:
            recv_a = lax.ppermute(send_a, "leaf", pairs_a)
            recv_xa = lax.ppermute(x_a, "leaf", pairs_a)
            parts.append(near_part((0, 1), emb, x_tree, hn))
            partner, parts[-1] = after((partner, parts[-1]))
        if stage == 2:
            recv_xb = lax.ppermute(x_b, "leaf", pairs_up + pairs_down)
            parts.append(near_part((2, 3), emb, x_tree, hn))
            partner, parts[-1], recv_up, recv_down = after(
                (partner, parts[-1], recv_up, recv_down)
            )
        if stage == 3:
            parts.append(near_part(tuple(range(4, leaves)), emb, x_tree, hn))
            partner, parts[-1], recv_a, recv_xa, recv_xb = after(
                (partner, parts[-1], recv_a, recv_xa, recv_xb)
            )
        if bit:
            block = join(block, partner, *([owned[level]] if level < LEVELS else []))
            block, x_tree, send_a, x_b = after((block, x_tree, send_a, x_b))

    table = []
    for lev, off, row in sorted(plan.entries, key=lambda e: e[2]):
        for i in range(plan.padded[lev]):
            side = (off >> plan.shift[lev]) & 1
            table.append(
                (
                    off,
                    (side * LEVELS + lev) * R + i,
                    (1 << plan.shift[lev]) - 1,
                    plan.slots[lev],
                    i < plan.slots[lev],
                )
            )
    table = jnp.array(table, jnp.int32).T
    own_w = LEVELS * R
    dest = table[1] + jnp.bitwise_and(pos ^ table[0], table[2]) * table[3]
    dest = jnp.where(table[4] == 1, dest, -1)[None, :]

    half = plan.size // 2

    def sorted_rows(first, dest_ref, *refs):
        at = lax.broadcasted_iota(jnp.int32, (own_w, half), 0)
        total = None
        for i, ref in enumerate(refs):
            d = dest_ref[:, i * half : (i + 1) * half] - first
            term = dot(jnp.where(at == d, 1.0, 0.0).astype(BF16), ref[...])
            total = term if total is None else total + term
        return total.astype(BF16)

    def own_kernel(block_ref, other_ref, dest_ref, emb_ref, x_ref, hn_ref, z_ref):
        sk = sorted_rows(0, dest_ref, block_ref, other_ref)
        hs = half_norm_col(sk)
        z = jnp.zeros((cols, own_w), F32)
        held = None
        for c in range(0, leaves, 2):
            sl = slice(c * LEAF, (c + 2) * LEAF)
            k = jnp.exp(dot(sk, emb_ref[:, sl]) - (hs + hn_ref[:, sl])).astype(BF16)
            if held is not None:
                z = z + dot_nt(x_ref[:, held[0]], held[1])
            held = (sl, k)
        z_ref[...] = z + dot_nt(x_ref[:, held[0]], held[1])

    z = call(
        own_kernel,
        jax.ShapeDtypeStruct((cols, own_w), F32),
        block,
        partner,
        dest,
        emb,
        x_tree,
        hn,
        flops=50 * 2 * 256**3,
        nbytes=4 << 20,
        name="own",
    )

    def far_kernel(block_ref, other_ref, dest_ref, emb_ref, hn_ref, out_ref):
        sk = sorted_rows(own_w, dest_ref, block_ref, other_ref)
        hs = half_norm_col(sk)
        for c in range(0, leaves, 2):
            sl = slice(c * LEAF, (c + 2) * LEAF)
            g = dot(sk, emb_ref[:, sl])
            out_ref[:, sl] = jnp.exp(g - (hs + hn_ref[:, sl])).astype(BF16)

    def far_part(block, partner, emb, hn):
        return call(
            far_kernel,
            jax.ShapeDtypeStruct((own_w, points), BF16),
            block,
            partner,
            dest,
            emb,
            hn,
            flops=30 * 2 * 256**3,
            nbytes=4 << 20,
            name="far",
        )

    def low_edge(mult_ref, emb_ref, hn_ref, src_ref, xs_ref, near_ref):
        acc = [jnp.zeros((cols, LEAF), F32)] * W
        for q in range(W):
            sq, sp = slice(q * LEAF, (q + 1) * LEAF), slice(0, (q + 1) * LEAF)
            es = src_ref[:, sq]
            g = dot(jnp.transpose(es), emb_ref[:, sp])
            k = jnp.exp(g - (col_of(half_norm_row(es)) + hn_ref[:, sp])).astype(BF16)
            y = dot(xs_ref[:, sq], k)
            for t in range(q + 1):
                acc[t] = acc[t] + mult_ref[t, q - t] * y[:, t * LEAF : (t + 1) * LEAF]
        near_ref[:, 0:halo] = jnp.concatenate(acc, axis=1)
        near_ref[:, halo:] = jnp.zeros((cols, points - halo), F32)

    def high_edge(mult_ref, emb_ref, hn_ref, src_ref, xs_ref, near_ref):
        acc = [jnp.zeros((cols, LEAF), F32)] * W
        for q in range(W):
            sq, sp = slice(q * LEAF, (q + 1) * LEAF), slice((leaves - W + q) * LEAF, points)
            es = src_ref[:, sq]
            g = dot(jnp.transpose(es), emb_ref[:, sp])
            k = jnp.exp(g - (col_of(half_norm_row(es)) + hn_ref[:, sp])).astype(BF16)
            y = dot(xs_ref[:, sq], k)
            for i in range(W - q):
                t = leaves - W + q + i
                acc[q + i] = acc[q + i] + (
                    mult_ref[t, leaves + q - t + W] * y[:, i * LEAF : (i + 1) * LEAF]
                )
        near_ref[:, 0 : points - halo] = jnp.zeros((cols, points - halo), F32)
        near_ref[:, points - halo :] = jnp.concatenate(acc, axis=1)

    def core_kernel(mult_ref, emb_ref, hn_ref, src_ref, xs_ref, near_ref):
        odd = jnp.bitwise_and(lax.axis_index("leaf"), 1)
        for code, edge in ((1, low_edge), (0, high_edge)):

            @pl.when(odd == code)
            def _():
                edge(mult_ref, emb_ref, hn_ref, src_ref, xs_ref, near_ref)

    def core_part(emb, hn):
        return call(
            core_kernel,
            jax.ShapeDtypeStruct((cols, points), F32),
            mult,
            emb,
            hn,
            recv_a,
            recv_xa,
            smem=(0,),
            flops=30 * 2 * 256**3,
            nbytes=3 << 20,
            name="edge_core",
        )

    def chip_kernel(mult_ref, emb_ref, hn_ref, x_ref, up_ref, down_ref, xs_ref, near_ref, back_ref):
        odd = jnp.bitwise_and(lax.axis_index("leaf"), 1)

        def kernel_of(es, sp):
            g = dot(jnp.transpose(es), emb_ref[:, sp])
            return jnp.exp(g - (col_of(half_norm_row(es)) + hn_ref[:, sp])).astype(BF16)

        def told(row):
            return xs_ref[cols + row : cols + row + 1, 0:LEAF].astype(F32)

        def leaf(q):
            return slice(q * LEAF, (q + 1) * LEAF)

        @pl.when(odd == 1)
        def _():
            k = kernel_of(down_ref[...], slice(last, points))
            y = dot(xs_ref[0:cols, 0:LEAF], k)
            back = jnp.zeros((cols, LEAF), F32)
            for q in range(W):
                t = leaves - W + q
                near_ref[:, leaf(t)] = mult_ref[t, 2 * W - q] * y[:, leaf(q)]
                back = back + told(W - 1 - q) * dot_nt(x_ref[:, leaf(t)], k[:, leaf(q)])
            near_ref[:, 0:last] = jnp.zeros((cols, last), F32)
            back_ref[:, leaf(0)] = back
            back_ref[:, leaf(1)] = jnp.zeros((cols, LEAF), F32)

        @pl.when(odd == 0)
        def _():
            k3 = kernel_of(up_ref[:, leaf(1)], slice(LEAF, 3 * LEAF))
            k2 = kernel_of(up_ref[:, leaf(0)], leaf(1))
            y3 = dot(xs_ref[0:cols, leaf(2)], k3)
            y2 = dot(xs_ref[0:cols, leaf(1)], k2)
            near_ref[:, leaf(0)] = jnp.zeros((cols, LEAF), F32)
            near_ref[:, leaf(1)] = mult_ref[1, 1] * y3[:, leaf(0)] + mult_ref[1, 0] * y2
            near_ref[:, leaf(2)] = mult_ref[2, 0] * y3[:, leaf(1)]
            near_ref[:, halo:] = jnp.zeros((cols, last), F32)
            back_ref[:, leaf(1)] = told(0) * dot_nt(x_ref[:, leaf(1)], k3[:, leaf(0)]) + told(
                1
            ) * dot_nt(x_ref[:, leaf(2)], k3[:, leaf(1)])
            back_ref[:, leaf(0)] = told(2) * dot_nt(x_ref[:, leaf(1)], k2)

    def chip_part(emb, hn):
        return call(
            chip_kernel,
            [
                jax.ShapeDtypeStruct((cols, points), F32),
                jax.ShapeDtypeStruct((cols, UP * LEAF), F32),
            ],
            mult,
            emb,
            hn,
            x_tree,
            recv_up,
            recv_down,
            recv_xb,
            smem=(0,),
            flops=30 * 2 * 256**3,
            nbytes=4 << 20,
            name="edge_chip",
        )

    level_of = lax.broadcasted_iota(jnp.int32, (1, own_w), 1) // R
    for stage, bit in enumerate(range(plan.bits)):
        heard = lax.ppermute(z, "leaf", [(i, i ^ (1 << bit)) for i in range(n)])
        if stage == 1:
            chip_near, back = chip_part(emb, hn)
            heard, chip_near, back = after((heard, chip_near, back))
        if stage == 2:
            back = lax.ppermute(back, "leaf", pairs_up + pairs_down)
            far_k = far_part(block, partner, emb, hn)
            heard, far_k = after((heard, far_k))
        if stage == 3:
            parts += [core_part(emb, hn), chip_near]
            heard, parts[-2] = after((heard, parts[-2]))
        swap = level_of == plan.bits - 1 - bit
        add = level_of < plan.bits - 1 - bit
        z = jnp.where(add, z + heard, jnp.where(swap, heard, z))
        z, emb = after((z, emb))

    def last_kernel(z_ref, core_ref, far_ref, back_ref, inv_ref, *rest):
        part_refs, out_ref = rest[:-1], rest[-1]
        me = lax.axis_index("leaf")
        weights = []
        for l in range(LEVELS):
            node = 2 ** (l + 1) - 2 + (jnp.right_shift(me, plan.shift[l]) ^ 1)
            weights.append(
                jnp.dot(
                    z_ref[:, l * R : (l + 1) * R],
                    core_ref[node],
                    precision=lax.Precision.HIGHEST,
                    preferred_element_type=F32,
                ).astype(BF16)
            )
        w = jnp.concatenate(weights, axis=1)
        tree = dot(w, far_ref[...])
        for ref in part_refs:
            tree = tree + ref[...]
        even = jnp.bitwise_and(me, 1) == 0
        low_back = jnp.where(even, back_ref[:, 0:LEAF], 0.0)
        high_back = jnp.where(even, 0.0, back_ref[...])
        tree = tree + jnp.concatenate(
            [low_back, jnp.zeros((cols, points - (1 + UP) * LEAF), F32), high_back], axis=1
        )
        top = tree.astype(BF16)
        rest = (tree - top.astype(F32)).astype(BF16)
        stack = jnp.concatenate(
            [
                jnp.concatenate([v[:, h * LANES : (h + 1) * LANES] for v in (top, rest)], axis=1)
                for h in range(groups)
            ],
            axis=0,
        )
        low = jnp.bitwise_and(inv_ref[...], LANES - 1)
        high = jnp.right_shift(inv_ref[...], LANES.bit_length() - 1)
        hot = jnp.where(
            lax.broadcasted_iota(jnp.int32, (LANES, points), 0) == low, 1.0, 0.0
        ).astype(BF16)
        for c in range(leaves):
            sl = slice(c * LEAF, (c + 1) * LEAF)
            y = dot(stack, jnp.concatenate([hot[:, sl]] * 2, axis=0))
            out = jnp.zeros((cols, LEAF), F32)
            for h in range(groups):
                out = out + jnp.where(high[:, sl] == h, y[h * cols : (h + 1) * cols], 0.0)
            out_ref[:, sl] = out

    return call(
        last_kernel,
        jax.ShapeDtypeStruct((cols, points), F32),
        z,
        core,
        far_k,
        back,
        inv,
        *parts,
        flops=30 * 2 * 256**3,
        nbytes=2 << 20,
        name="last",
    )


def solution(mesh):
    return jax.shard_map(
        body,
        mesh=mesh,
        in_specs=(
            P(None, ("groups", "leaf")),
            P(None, ("groups", "leaf")),
            P(("groups", "leaf"), None),
            P(("groups", "leaf"), None),
            P(("groups", "leaf"), None),
            P("groups", None),
            P("groups", None, None),
        ),
        out_specs=P(None, ("groups", "leaf")),
        check_vma=False,
    )
```

```python
import jax
import jax.numpy as jnp
from jax import lax
from jax.experimental import pallas as pl
from jax.experimental.pallas import tpu as pltpu
from jax.sharding import PartitionSpec as P

LEAF = 256
R = 64
LEVELS = 4
W = 3
F32 = jnp.float32
BF16 = jnp.bfloat16
VMEM_LIMIT = 14 * 1024 * 1024
LANES = 128
PREP_VMEM = 16 * 1024 * 1024
UP = 2


def dot(a, b):
    return jnp.dot(a, b, preferred_element_type=F32)


def dot_nt(a, b):
    return lax.dot_general(a, b, (((1,), (1,)), ((), ())), preferred_element_type=F32)


def dot_tn(a, b):
    return lax.dot_general(a, b, (((0,), (0,)), ((), ())), preferred_element_type=F32)


def half_norm_row(emb):
    e = emb.astype(F32)
    return 0.5 * jnp.sum(e * e, axis=0, keepdims=True)


def half_norm_col(rows):
    e = rows.astype(F32)
    return 0.5 * jnp.sum(e * e, axis=1, keepdims=True)


def col_of(row):
    return jnp.transpose(jnp.broadcast_to(row, (8, row.shape[1])))[:, 0:1]


def call(kernel, outs, *args, scratch=(), smem=(), hbm=(), flops=0, nbytes=0, name=None, vmem=VMEM_LIMIT):
    single = not isinstance(outs, (list, tuple))
    vm = pl.BlockSpec(memory_space=pltpu.VMEM)
    sm = pl.BlockSpec(memory_space=pltpu.SMEM)
    hb = pl.BlockSpec(memory_space=pltpu.HBM)
    return pl.pallas_call(
        kernel,
        out_shape=outs,
        in_specs=[sm if i in smem else hb if i in hbm else vm for i in range(len(args))],
        out_specs=vm if single else [vm] * len(outs),
        scratch_shapes=list(scratch),
        compiler_params=pltpu.CompilerParams(vmem_limit_bytes=vmem),
        cost_estimate=pl.CostEstimate(flops=0, bytes_accessed=0, transcendentals=0),
        name=name,
    )(*args)


class Plan:
    def __init__(self, n):
        self.n = n
        self.bits = n.bit_length() - 1
        self.slots = [R * 2 ** (l + 1) // n for l in range(LEVELS)]
        self.padded = [-(-s // 8) * 8 for s in self.slots]
        self.starts = [sum(self.padded[:l]) for l in range(LEVELS)]
        self.rows = sum(self.padded)
        self.shift = [self.bits - 1 - l for l in range(LEVELS)]
        entries, size = [], 0
        for bit in reversed(range(self.bits)):
            level = self.bits - 1 - bit
            if level < LEVELS:
                entries.append((level, 0, size))
                size += self.padded[level]
            entries += [(lev, off ^ (1 << bit), row + size) for lev, off, row in entries]
            size *= 2
        self.entries, self.size = entries, size


def body(embeddings, probes, order, near_list, near_count, skeleton, core):
    n = lax.axis_size("leaf")
    plan = Plan(n)
    pos = lax.axis_index("leaf")
    width, points = embeddings.shape
    cols = probes.shape[0]
    leaves = points // LEAF
    halo = W * LEAF

    groups = points // LANES
    last = points - halo
    extra = 16
    slabs = 4
    slab = width // slabs
    reach = 2 * W + 1

    pairs_a = [(i, i ^ 1) for i in range(n)]

    def pairs(*starts):
        up = [(i, i + 1) for at in starts for i in range(at, n - 1, 4)]
        return up + [(j, i) for i, j in up]

    def cut_kernel(emb_ref, x_ref, a_ref, sem):
        odd = jnp.bitwise_and(lax.axis_index("leaf"), 1)
        at = pl.multiple_of((1 - odd) * last, LEAF)
        copy = pltpu.make_async_copy(
            emb_ref.at[:, pl.ds(at, halo)], a_ref.at[pl.ds(0, width), :], sem.at[0]
        )
        copy.start()
        ends = jnp.where(odd == 1, x_ref[:, :halo].astype(F32), x_ref[:, last:].astype(F32))
        a_ref[width:, :] = ends.astype(BF16)
        copy.wait()

    def cut_core(emb, x_tree):
        return call(
            cut_kernel,
            jax.ShapeDtypeStruct((width + cols, halo), BF16),
            emb,
            x_tree,
            scratch=[pltpu.SemaphoreType.DMA((1,))],
            name="cut",
        )

    def fill(b_ref, x_ref, mult_ref):
        odd = jnp.bitwise_and(lax.axis_index("leaf"), 1)

        def tell(pairs):
            rows = [mult_ref[(o + W) * leaves + t : (o + W) * leaves + t + 1, :] for t, o in pairs]
            rows.append(jnp.zeros((extra - len(rows), LANES), F32))
            b_ref[width + cols :, 0:LANES] = jnp.concatenate(rows, axis=0).astype(BF16)
            b_ref[width + cols :, LANES:] = jnp.zeros((extra, UP * LEAF - LANES), BF16)

        @pl.when(odd == 0)
        def _():
            b_ref[width : width + cols, :] = x_ref[:, : UP * LEAF]
            tell([(0, -1 - q) for q in range(W)])

        @pl.when(odd == 1)
        def _():
            b_ref[width : width + cols, :] = x_ref[:, points - UP * LEAF :]
            tell([(leaves - 1, 2), (leaves - 1, 3), (leaves - 2, 3)])

    def cut_chip_kernel(emb_ref, x_ref, mult_ref, b_ref, sem):
        odd = jnp.bitwise_and(lax.axis_index("leaf"), 1)
        at = pl.multiple_of(odd * (points - UP * LEAF), LEAF)
        copy = pltpu.make_async_copy(
            emb_ref.at[:, pl.ds(at, UP * LEAF)], b_ref.at[pl.ds(0, width), :], sem.at[0]
        )
        copy.start()
        fill(b_ref, x_ref, mult_ref)
        copy.wait()

    def cut_chip(emb, x_tree):
        return call(
            cut_chip_kernel,
            jax.ShapeDtypeStruct((width + cols + extra, UP * LEAF), BF16),
            emb,
            x_tree,
            mult,
            scratch=[pltpu.SemaphoreType.DMA((1,))],
            name="cut_chip",
        )

    def prep_kernel(
        skel_hbm, order_hbm, probes_hbm, list_hbm, count_hbm, emb_hbm, *rest
    ):
        g_refs, rest = rest[:LEVELS], rest[LEVELS:]
        x_ref, inv_ref, hn_ref, mult_ref = rest[:4]
        emb_ref, skel_ref, order_ref, probes_ref, list_ref, count_ref, row_ref, sems = rest[4:]
        me = lax.axis_index("leaf")
        small = [
            pltpu.make_async_copy(src, dst, sems.at[i])
            for i, (src, dst) in enumerate(
                (
                    (skel_hbm, skel_ref),
                    (order_hbm, order_ref),
                    (probes_hbm, probes_ref),
                    (list_hbm, list_ref),
                    (count_hbm, count_ref),
                )
            )
        ]
        large = [
            pltpu.make_async_copy(
                emb_hbm.at[pl.ds(r * slab, slab), :], emb_ref.at[pl.ds(r * slab, slab), :], sems.at[5 + r]
            )
            for r in range(slabs)
        ]
        for copy in small + large:
            copy.start()
        for copy in small:
            copy.wait()

        lane = lax.broadcasted_iota(jnp.int32, (1, LANES), 1)
        idx = jnp.full((1, LANES), -1, jnp.int32)
        row_ref[...] = jnp.zeros_like(row_ref)
        for l in range(LEVELS):
            node = 2 ** (l + 1) - 2 + jnp.right_shift(me, plan.shift[l])
            row_ref[0:1, 0:R] = skel_ref[pl.ds(node, 1), :]
            within = jnp.bitwise_and(me, (1 << plan.shift[l]) - 1)
            shift = jnp.bitwise_and(plan.starts[l] - within * plan.slots[l] + LANES, LANES - 1)
            rolled = pltpu.roll(row_ref[...], shift, 1)[0:1, :]
            mine = (lane >= plan.starts[l]) & (lane < plan.starts[l] + plan.slots[l])
            idx = jnp.where(mine, rolled - me * points, idx)
        pick = jnp.where(
            lax.broadcasted_iota(jnp.int32, (points, LANES), 0) == idx, 1.0, 0.0
        ).astype(BF16)

        near = list_ref[...]
        slots = near.shape[1]
        sub = lax.broadcasted_iota(jnp.int32, (leaves, leaves), 0)
        here = sub == lax.broadcasted_iota(jnp.int32, (leaves, leaves), 1)
        count = jnp.sum(jnp.where(here, count_ref[...], 0), axis=1, keepdims=True)
        alive = lax.broadcasted_iota(jnp.int32, (leaves, slots), 1) < count
        offset = near - (me * leaves + lax.broadcasted_iota(jnp.int32, (leaves, slots), 0))
        for o in range(reach):
            hits = jnp.where(alive & (offset == o - W), 1.0, 0.0)
            mult_ref[o * leaves : (o + 1) * leaves, :] = jnp.broadcast_to(
                jnp.sum(hits, axis=1, keepdims=True), (leaves, LANES)
            )

        order_row = order_ref[...]
        low = jnp.bitwise_and(order_row, LANES - 1)
        high = jnp.right_shift(order_row, LANES.bit_length() - 1)
        hot = jnp.where(
            lax.broadcasted_iota(jnp.int32, (LANES, points), 0) == low, 1.0, 0.0
        ).astype(BF16)
        stack = jnp.concatenate(
            [probes_ref[:, h * LANES : (h + 1) * LANES] for h in range(groups)], axis=0
        )
        for c in range(leaves):
            sl = slice(c * LEAF, (c + 1) * LEAF)
            y = dot(stack, hot[:, sl])
            x = jnp.zeros((cols, LEAF), F32)
            for h in range(groups):
                x = x + jnp.where(high[:, sl] == h, y[h * cols : (h + 1) * cols], 0.0)
            x_ref[:, sl] = x.astype(BF16)

        k = lax.broadcasted_iota(jnp.int32, (8, points), 1)
        first = lax.broadcasted_iota(jnp.int32, (8, points), 0) == 0
        digits = jnp.where(first, jnp.right_shift(k, 4), jnp.bitwise_and(k, 15)).astype(F32)
        spread = jnp.concatenate(
            [jnp.where(high == h, digits, 0.0) for h in range(groups)], axis=0
        ).astype(BF16)
        found = dot_nt(spread, hot)
        for h in range(groups):
            inv_ref[:, h * LANES : (h + 1) * LANES] = (
                found[8 * h : 8 * h + 1] * 16.0 + found[8 * h + 1 : 8 * h + 2]
            ).astype(jnp.int32)

        hn = jnp.zeros((1, points), F32)
        for r in range(slabs):
            large[r].wait()
            rows = slice(r * slab, (r + 1) * slab)
            picked = jnp.transpose(dot(emb_ref[rows, :], pick))
            for l in range(LEVELS):
                g_refs[l][:, rows] = picked[
                    plan.starts[l] : plan.starts[l] + plan.padded[l]
                ].astype(BF16)
            hn = hn + half_norm_row(emb_ref[rows, :])
        hn_ref[...] = hn

    *owned, x_tree, inv, hn, mult = call(
        prep_kernel,
        [jax.ShapeDtypeStruct((p, width), BF16) for p in plan.padded]
        + [
            jax.ShapeDtypeStruct((cols, points), BF16),
            jax.ShapeDtypeStruct((1, points), jnp.int32),
            jax.ShapeDtypeStruct((1, points), F32),
            jax.ShapeDtypeStruct((reach * leaves, LANES), F32),
        ],
        *[pltpu.with_memory_space_constraint(v, pltpu.HBM) for v in (skeleton, order, probes, near_list, near_count)],
        pltpu.with_memory_space_constraint(embeddings, pltpu.HBM),
        hbm=tuple(range(6)),
        scratch=[
            pltpu.VMEM((width, points), BF16),
            pltpu.VMEM(skeleton.shape, jnp.int32),
            pltpu.VMEM(order.shape, jnp.int32),
            pltpu.VMEM(probes.shape, BF16),
            pltpu.VMEM(near_list.shape, jnp.int32),
            pltpu.VMEM(near_count.shape, jnp.int32),
            pltpu.VMEM((8, LANES), jnp.int32),
            pltpu.SemaphoreType.DMA((6 + slabs,)),
        ],
        flops=50 * 2 * 256**3,
        nbytes=6 << 20,
        name="prep",
        vmem=PREP_VMEM,
    )

    emb, x_tree = lax.optimization_barrier((embeddings, x_tree))

    def times(mult_ref, t, o, value):
        row = mult_ref[o * leaves + t : o * leaves + t + 1, :]
        return value * jnp.concatenate([row] * (LEAF // LANES), axis=1)

    def near_kernel(rows, mult_ref, emb_ref, x_ref, hn_ref, *rest):
        near_ref = rest[-1]
        acc = [None] * leaves

        def add(j, value):
            acc[j] = value if acc[j] is None else acc[j] + value

        def make(i):
            w = min(W + 1, leaves - i)
            si, sp = slice(i * LEAF, (i + 1) * LEAF), slice(i * LEAF, (i + w) * LEAF)
            g = dot(jnp.transpose(emb_ref[:, si]), emb_ref[:, sp])
            return jnp.exp(g - (col_of(hn_ref[:, si]) + hn_ref[:, sp])).astype(BF16)

        def use(i, k):
            y = dot(x_ref[:, i * LEAF : (i + 1) * LEAF], k)
            for q in range(k.shape[1] // LEAF):
                j = i + q
                sq = slice(q * LEAF, (q + 1) * LEAF)
                add(j, times(mult_ref, j, W - q, y[:, sq]))
                if q:
                    sj = slice(j * LEAF, (j + 1) * LEAF)
                    add(i, times(mult_ref, i, W + q, dot_nt(x_ref[:, sj], k[:, sq])))

        held = None
        for i in rows:
            k = make(i)
            if held is not None:
                use(*held)
            held = (i, k)
        use(*held)
        for j in range(leaves):
            sj = slice(j * LEAF, (j + 1) * LEAF)
            if len(rest) > 1:
                add(j, rest[0][:, sj])
            near_ref[:, sj] = jnp.zeros((cols, LEAF), F32) if acc[j] is None else acc[j]

    def near_part(rows, emb, x_tree, hn, *near):
        return call(
            lambda *refs: near_kernel(rows, *refs),
            jax.ShapeDtypeStruct((cols, points), F32),
            mult,
            emb,
            x_tree,
            hn,
            *near,
            flops=60 * 2 * 256**3,
            nbytes=6 << 20,
            name="near%d" % rows[0],
        )

    def low_edge(mult_ref, emb_ref, hn_ref, src_ref, near_in, near_ref):
        acc = [jnp.zeros((cols, LEAF), F32)] * W
        for q in range(W):
            sq, sp = slice(q * LEAF, (q + 1) * LEAF), slice(0, (q + 1) * LEAF)
            es = src_ref[0:width, sq]
            g = dot(jnp.transpose(es), emb_ref[:, sp])
            k = jnp.exp(g - (col_of(half_norm_row(es)) + hn_ref[:, sp])).astype(BF16)
            y = dot(src_ref[width:, sq], k)
            for t in range(q + 1):
                acc[t] = acc[t] + times(mult_ref, t, q - t, y[:, t * LEAF : (t + 1) * LEAF])
        near_ref[:, 0:halo] = near_in[:, 0:halo] + jnp.concatenate(acc, axis=1)
        near_ref[:, halo:] = near_in[:, halo:]

    def high_edge(mult_ref, emb_ref, hn_ref, src_ref, near_in, near_ref):
        acc = [jnp.zeros((cols, LEAF), F32)] * W
        for q in range(W):
            sq, sp = slice(q * LEAF, (q + 1) * LEAF), slice((leaves - W + q) * LEAF, points)
            es = src_ref[0:width, sq]
            g = dot(jnp.transpose(es), emb_ref[:, sp])
            k = jnp.exp(g - (col_of(half_norm_row(es)) + hn_ref[:, sp])).astype(BF16)
            y = dot(src_ref[width:, sq], k)
            for i in range(W - q):
                t = leaves - W + q + i
                acc[q + i] = acc[q + i] + (
                    times(mult_ref, t, leaves + q - t + W, y[:, i * LEAF : (i + 1) * LEAF])
                )
        near_ref[:, 0:last] = near_in[:, 0:last]
        near_ref[:, last:] = near_in[:, last:] + jnp.concatenate(acc, axis=1)

    def core_kernel(mult_ref, emb_ref, hn_ref, src_ref, near_in, near_ref):
        odd = jnp.bitwise_and(lax.axis_index("leaf"), 1)
        for code, edge in ((1, low_edge), (0, high_edge)):

            @pl.when(odd == code)
            def _():
                edge(mult_ref, emb_ref, hn_ref, src_ref, near_in, near_ref)

    def core_part(emb, hn, recv_a, near):
        return call(
            core_kernel,
            jax.ShapeDtypeStruct((cols, points), F32),
            mult,
            emb,
            hn,
            recv_a,
            near,
            flops=30 * 2 * 256**3,
            nbytes=3 << 20,
            name="edge_core",
        )

    def kernel_of(es, emb_ref, hn_ref, sp):
        g = dot(jnp.transpose(es), emb_ref[:, sp])
        return jnp.exp(g - (col_of(half_norm_row(es)) + hn_ref[:, sp])).astype(BF16)

    def told(src_ref, row, value):
        at = width + cols + row
        count = src_ref[at : at + 1, 0:LANES].astype(F32)
        return value * jnp.concatenate([count] * (LEAF // LANES), axis=1)

    def leaf(q):
        return slice(q * LEAF, (q + 1) * LEAF)

    def upper(mult_ref, emb_ref, hn_ref, x_ref, src_ref, near_ref, back_ref):
        k3 = kernel_of(src_ref[0:width, leaf(1)], emb_ref, hn_ref, slice(LEAF, 3 * LEAF))
        k2 = kernel_of(src_ref[0:width, leaf(0)], emb_ref, hn_ref, leaf(1))
        y3 = dot(src_ref[width : width + cols, leaf(1)], k3)
        y2 = dot(src_ref[width : width + cols, leaf(0)], k2)
        near_ref[:, leaf(1)] += times(mult_ref, 1, 1, y3[:, leaf(0)]) + times(mult_ref, 1, 0, y2)
        near_ref[:, leaf(2)] += times(mult_ref, 2, 0, y3[:, leaf(1)])
        back_ref[:, leaf(0)] = told(src_ref, 2, dot_nt(x_ref[:, leaf(1)], k2))
        back_ref[:, leaf(1)] = told(src_ref, 0, dot_nt(x_ref[:, leaf(1)], k3[:, leaf(0)])) + told(
            src_ref, 1, dot_nt(x_ref[:, leaf(2)], k3[:, leaf(1)])
        )

    def lower(mult_ref, emb_ref, hn_ref, x_ref, src_ref, near_ref, back_ref):
        k = kernel_of(src_ref[0:width, leaf(0)], emb_ref, hn_ref, slice(last, points))
        y = dot(src_ref[width : width + cols, leaf(0)], k)
        back = jnp.zeros((cols, LEAF), F32)
        for q in range(W):
            t = leaves - W + q
            near_ref[:, leaf(t)] += times(mult_ref, t, 2 * W - q, y[:, leaf(q)])
            back = back + told(src_ref, W - 1 - q, dot_nt(x_ref[:, leaf(t)], k[:, leaf(q)]))
        back_ref[:, leaf(0)] = back
        back_ref[:, leaf(1)] = jnp.zeros((cols, LEAF), F32)

    def chip_kernel(mult_ref, emb_ref, hn_ref, x_ref, one_ref, two_ref, near_in, near_ref, back_ref):
        near_ref[...] = near_in[...]
        turn = jnp.bitwise_and(lax.axis_index("leaf"), 3)
        for code, side, src_ref in (
            (1, lower, one_ref),
            (2, upper, one_ref),
            (3, lower, two_ref),
            (0, upper, two_ref),
        ):

            @pl.when(turn == code)
            def _():
                side(mult_ref, emb_ref, hn_ref, x_ref, src_ref, near_ref, back_ref)

    def chip_part(emb, recv_b1, recv_b2, near):
        return call(
            chip_kernel,
            [
                jax.ShapeDtypeStruct((cols, points), F32),
                jax.ShapeDtypeStruct((cols, UP * LEAF), F32),
            ],
            mult,
            emb,
            hn,
            x_tree,
            recv_b1,
            recv_b2,
            near,
            name="edge_chip",
        )

    table = []
    for lev, off, row in sorted(plan.entries, key=lambda e: e[2]):
        for i in range(plan.padded[lev]):
            side = (off >> plan.shift[lev]) & 1
            table.append(
                (
                    off,
                    (side * LEVELS + lev) * R + i,
                    (1 << plan.shift[lev]) - 1,
                    plan.slots[lev],
                    i < plan.slots[lev],
                )
            )
    table = jnp.array(table, jnp.int32).T
    own_w = LEVELS * R
    dest = table[1] + jnp.bitwise_and(pos ^ table[0], table[2]) * table[3]
    dest = jnp.where(table[4] == 1, dest, -1)[None, :]

    def join_kernel(*refs):
        row = 0
        for ref in refs[:-1]:
            refs[-1][row : row + ref.shape[0], :] = ref[...]
            row += ref.shape[0]

    def join(*blocks):
        rows = sum(v.shape[0] for v in blocks)
        return call(
            join_kernel, jax.ShapeDtypeStruct((rows, width), BF16), *blocks, nbytes=1 << 18, name="join"
        )

    after = lax.optimization_barrier
    block = owned[0]
    for bit in reversed(range(plan.bits)):
        level = plan.bits - bit
        stage = level - 1
        partner = lax.ppermute(block, "leaf", [(i, i ^ (1 << bit)) for i in range(n)])
        if stage == 0:
            partner, x_tree, dest = after((partner, x_tree, dest))
        if stage == 1:
            near = near_part((0, 1), emb, x_tree, hn)
            send_a = cut_core(emb, x_tree)
            partner, near, send_a = after((partner, near, send_a))
        if stage == 2:
            recv_a = lax.ppermute(send_a, "leaf", pairs_a)
            near = near_part((2, 3), emb, x_tree, hn, near)
            partner, near = after((partner, near))
        if stage == 3:
            near = near_part(tuple(range(4, leaves)), emb, x_tree, hn, near)
            emb, near = after((emb, near))
            recv_b2 = lax.ppermute(cut_chip(emb, x_tree), "leaf", pairs(3))
            near = core_part(emb, hn, recv_a, near)
            partner, near = after((partner, near))
        if bit:
            block = join(block, partner, *([owned[level]] if level < LEVELS else []))
            block, x_tree, emb = after((block, x_tree, emb))
    half = plan.size // 2

    def sorted_rows(first, dest_ref, *refs):
        at = lax.broadcasted_iota(jnp.int32, (own_w, half), 0)
        total = None
        for i, ref in enumerate(refs):
            d = dest_ref[:, i * half : (i + 1) * half] - first
            term = dot(jnp.where(at == d, 1.0, 0.0).astype(BF16), ref[...])
            total = term if total is None else total + term
        return total.astype(BF16)

    def own_kernel(block_ref, other_ref, dest_ref, emb_ref, x_ref, hn_ref, z_ref):
        sk = sorted_rows(0, dest_ref, block_ref, other_ref)
        hs = half_norm_col(sk)
        z = jnp.zeros((cols, own_w), F32)
        held = None
        for c in range(0, leaves, 2):
            sl = slice(c * LEAF, (c + 2) * LEAF)
            k = jnp.exp(dot(sk, emb_ref[:, sl]) - (hs + hn_ref[:, sl])).astype(BF16)
            if held is not None:
                z = z + dot_nt(x_ref[:, held[0]], held[1])
            held = (sl, k)
        z_ref[...] = z + dot_nt(x_ref[:, held[0]], held[1])

    z = call(
        own_kernel,
        jax.ShapeDtypeStruct((cols, own_w), F32),
        block,
        partner,
        dest,
        emb,
        x_tree,
        hn,
        flops=50 * 2 * 256**3,
        nbytes=4 << 20,
        name="own",
    )

    def far_kernel(block_ref, other_ref, dest_ref, emb_ref, hn_ref, out_ref):
        sk = sorted_rows(own_w, dest_ref, block_ref, other_ref)
        hs = half_norm_col(sk)
        for c in range(0, leaves, 2):
            sl = slice(c * LEAF, (c + 2) * LEAF)
            g = dot(sk, emb_ref[:, sl])
            out_ref[:, sl] = jnp.exp(g - (hs + hn_ref[:, sl])).astype(BF16)

    def far_part(block, partner, emb, hn):
        return call(
            far_kernel,
            jax.ShapeDtypeStruct((own_w, points), BF16),
            block,
            partner,
            dest,
            emb,
            hn,
            flops=30 * 2 * 256**3,
            nbytes=4 << 20,
            name="far",
        )

    level_of = lax.broadcasted_iota(jnp.int32, (1, own_w), 1) // R
    for stage, bit in enumerate([0] + list(range(3, plan.bits)) + [2, 1]):
        heard = lax.ppermute(z, "leaf", [(i, i ^ (1 << bit)) for i in range(n)])
        if stage == 0:
            far_k = far_part(block, partner, emb, hn)
            heard, far_k, recv_b2 = after((heard, far_k, recv_b2))
        if stage == 0:
            recv_b1 = lax.ppermute(cut_chip(emb, x_tree), "leaf", pairs(1))
        if stage == 3:
            near, back = chip_part(emb, recv_b1, recv_b2, near)
            heard, near, back = after((heard, near, back))
        if stage == 4:
            back = lax.ppermute(back, "leaf", pairs(1, 3))
        swap = level_of == plan.bits - 1 - bit
        add = level_of < plan.bits - 1 - bit
        z = jnp.where(add, z + heard, jnp.where(swap, heard, z))
        z, emb = after((z, emb))

    def last_kernel(z_ref, core_ref, far_ref, back_ref, inv_ref, near_ref, out_ref):
        me = lax.axis_index("leaf")
        weights = []
        for l in range(LEVELS):
            node = 2 ** (l + 1) - 2 + (jnp.right_shift(me, plan.shift[l]) ^ 1)
            weights.append(
                jnp.dot(
                    z_ref[:, l * R : (l + 1) * R],
                    core_ref[node],
                    precision=lax.Precision.HIGHEST,
                    preferred_element_type=F32,
                ).astype(BF16)
            )
        w = jnp.concatenate(weights, axis=1)
        tree = near_ref[...] + dot(w, far_ref[...])
        even = jnp.bitwise_and(me, 1) == 0
        low_back = jnp.where(even, back_ref[:, 0:LEAF], 0.0)
        high_back = jnp.where(even, 0.0, back_ref[...])
        tree = tree + jnp.concatenate(
            [low_back, jnp.zeros((cols, points - (1 + UP) * LEAF), F32), high_back], axis=1
        )
        top = tree.astype(BF16)
        rest = (tree - top.astype(F32)).astype(BF16)
        stack = jnp.concatenate(
            [
                jnp.concatenate([v[:, h * LANES : (h + 1) * LANES] for v in (top, rest)], axis=1)
                for h in range(groups)
            ],
            axis=0,
        )
        low = jnp.bitwise_and(inv_ref[...], LANES - 1)
        high = jnp.right_shift(inv_ref[...], LANES.bit_length() - 1)
        hot = jnp.where(
            lax.broadcasted_iota(jnp.int32, (LANES, points), 0) == low, 1.0, 0.0
        ).astype(BF16)
        for c in range(leaves):
            sl = slice(c * LEAF, (c + 1) * LEAF)
            y = dot(stack, jnp.concatenate([hot[:, sl]] * 2, axis=0))
            out = jnp.zeros((cols, LEAF), F32)
            for h in range(groups):
                out = out + jnp.where(high[:, sl] == h, y[h * cols : (h + 1) * cols], 0.0)
            out_ref[:, sl] = out

    return call(
        last_kernel,
        jax.ShapeDtypeStruct((cols, points), F32),
        z,
        core,
        far_k,
        back,
        inv,
        near,
        flops=30 * 2 * 256**3,
        nbytes=2 << 20,
        name="last",
    )


def solution(mesh):
    return jax.shard_map(
        body,
        mesh=mesh,
        in_specs=(
            P(None, ("groups", "leaf")),
            P(None, ("groups", "leaf")),
            P(("groups", "leaf"), None),
            P(("groups", "leaf"), None),
            P(("groups", "leaf"), None),
            P("groups", None),
            P("groups", None, None),
        ),
        out_specs=P(None, ("groups", "leaf")),
        check_vma=False,
    )
```

```python
import jax
import jax.numpy as jnp
from jax import lax
from jax.experimental import pallas as pl
from jax.experimental.pallas import tpu as pltpu
from jax.sharding import PartitionSpec as P

LEAF = 256
R = 64
LEVELS = 4
W = 3
F32 = jnp.float32
BF16 = jnp.bfloat16
VMEM_LIMIT = 14 * 1024 * 1024
LANES = 128
PREP_VMEM = 16 * 1024 * 1024
UP = 2


def dot(a, b):
    return jnp.dot(a, b, preferred_element_type=F32)


def dot_nt(a, b):
    return lax.dot_general(a, b, (((1,), (1,)), ((), ())), preferred_element_type=F32)


def dot_tn(a, b):
    return lax.dot_general(a, b, (((0,), (0,)), ((), ())), preferred_element_type=F32)


def half_norm_row(emb):
    e = emb.astype(F32)
    return 0.5 * jnp.sum(e * e, axis=0, keepdims=True)


def half_norm_col(rows):
    e = rows.astype(F32)
    return 0.5 * jnp.sum(e * e, axis=1, keepdims=True)


def col_of(row):
    return jnp.transpose(jnp.broadcast_to(row, (8, row.shape[1])))[:, 0:1]


def call(kernel, outs, *args, scratch=(), smem=(), hbm=(), flops=0, nbytes=0, name=None, vmem=VMEM_LIMIT, cost=0):
    single = not isinstance(outs, (list, tuple))
    vm = pl.BlockSpec(memory_space=pltpu.VMEM)
    sm = pl.BlockSpec(memory_space=pltpu.SMEM)
    hb = pl.BlockSpec(memory_space=pltpu.HBM)
    return pl.pallas_call(
        kernel,
        out_shape=outs,
        in_specs=[sm if i in smem else hb if i in hbm else vm for i in range(len(args))],
        out_specs=vm if single else [vm] * len(outs),
        scratch_shapes=list(scratch),
        compiler_params=pltpu.CompilerParams(vmem_limit_bytes=vmem),
        cost_estimate=pl.CostEstimate(flops=cost, bytes_accessed=0, transcendentals=0),
        name=name,
    )(*args)


class Plan:
    def __init__(self, n):
        self.n = n
        self.bits = n.bit_length() - 1
        self.slots = [R * 2 ** (l + 1) // n for l in range(LEVELS)]
        self.padded = [-(-s // 8) * 8 for s in self.slots]
        self.starts = [sum(self.padded[:l]) for l in range(LEVELS)]
        self.rows = sum(self.padded)
        self.shift = [self.bits - 1 - l for l in range(LEVELS)]
        entries, size = [], 0
        for bit in reversed(range(self.bits)):
            level = self.bits - 1 - bit
            if level < LEVELS:
                entries.append((level, 0, size))
                size += self.slots[level]
            entries += [(lev, off ^ (1 << bit), row + size) for lev, off, row in entries]
            size *= 2
        self.entries, self.size = entries, size


def body(embeddings, probes, order, near_list, near_count, skeleton, core):
    n = lax.axis_size("leaf")
    plan = Plan(n)
    pos = lax.axis_index("leaf")
    width, points = embeddings.shape
    cols = probes.shape[0]
    leaves = points // LEAF
    halo = W * LEAF

    groups = points // LANES
    last = points - halo
    extra = 8
    slabs = 4
    slab = width // slabs
    reach = 2 * W + 1

    pairs_a = [(i, i ^ 1) for i in range(n)]

    def pairs(*starts):
        up = [(i, i + 1) for at in starts for i in range(at, n - 1, 4)]
        return up + [(j, i) for i, j in up]

    def cut_kernel(emb_ref, x_ref, a_ref, sem):
        odd = jnp.bitwise_and(lax.axis_index("leaf"), 1)
        at = pl.multiple_of((1 - odd) * last, LEAF)
        copy = pltpu.make_async_copy(
            emb_ref.at[:, pl.ds(at, halo)], a_ref.at[pl.ds(0, width), :], sem.at[0]
        )
        copy.start()
        ends = jnp.where(odd == 1, x_ref[:, :halo].astype(F32), x_ref[:, last:].astype(F32))
        a_ref[width:, :] = ends.astype(BF16)
        copy.wait()

    def cut_core(emb, x_tree):
        return call(
            cut_kernel,
            jax.ShapeDtypeStruct((width + cols, halo), BF16),
            emb,
            x_tree,
            scratch=[pltpu.SemaphoreType.DMA((1,))],
            name="cut",
        )

    def fill(b_ref, x_ref, mult_ref):
        odd = jnp.bitwise_and(lax.axis_index("leaf"), 1)

        def tell(pairs):
            rows = [mult_ref[(o + W) * leaves + t : (o + W) * leaves + t + 1, :] for t, o in pairs]
            rows.append(jnp.zeros((extra - len(rows), LANES), F32))
            b_ref[width + cols :, 0:LANES] = jnp.concatenate(rows, axis=0).astype(BF16)
            b_ref[width + cols :, LANES:] = jnp.zeros((extra, UP * LEAF - LANES), BF16)

        @pl.when(odd == 0)
        def _():
            b_ref[width : width + cols, :] = x_ref[:, : UP * LEAF]
            tell([(0, -1 - q) for q in range(W)])

        @pl.when(odd == 1)
        def _():
            b_ref[width : width + cols, :] = x_ref[:, points - UP * LEAF :]
            tell([(leaves - 1, 2), (leaves - 1, 3), (leaves - 2, 3)])

    def cut_chip_kernel(emb_ref, x_ref, mult_ref, b_ref, sem):
        odd = jnp.bitwise_and(lax.axis_index("leaf"), 1)
        at = pl.multiple_of(odd * (points - UP * LEAF), LEAF)
        copy = pltpu.make_async_copy(
            emb_ref.at[:, pl.ds(at, UP * LEAF)], b_ref.at[pl.ds(0, width), :], sem.at[0]
        )
        copy.start()
        fill(b_ref, x_ref, mult_ref)
        copy.wait()

    def cut_chip(emb, x_tree):
        return call(
            cut_chip_kernel,
            jax.ShapeDtypeStruct((width + cols + extra, UP * LEAF), BF16),
            emb,
            x_tree,
            mult,
            scratch=[pltpu.SemaphoreType.DMA((1,))],
            name="cut_chip",
        )

    def prep_kernel(skel_hbm, emb_hbm, *rest):
        g_refs, (emb_ref, skel_ref, row_ref, sems) = rest[:LEVELS], rest[LEVELS:]
        me = lax.axis_index("leaf")
        small = pltpu.make_async_copy(skel_hbm, skel_ref, sems.at[slabs])
        large = [
            pltpu.make_async_copy(
                emb_hbm.at[pl.ds(r * slab, slab), :], emb_ref.at[pl.ds(r * slab, slab), :], sems.at[r]
            )
            for r in range(slabs)
        ]
        for copy in [small] + large:
            copy.start()
        small.wait()

        lane = lax.broadcasted_iota(jnp.int32, (1, LANES), 1)
        idx = jnp.full((1, LANES), -1, jnp.int32)
        row_ref[...] = jnp.zeros_like(row_ref)
        for l in range(LEVELS):
            node = 2 ** (l + 1) - 2 + jnp.right_shift(me, plan.shift[l])
            row_ref[0:1, 0:R] = skel_ref[pl.ds(node, 1), :]
            within = jnp.bitwise_and(me, (1 << plan.shift[l]) - 1)
            shift = jnp.bitwise_and(plan.starts[l] - within * plan.slots[l] + LANES, LANES - 1)
            rolled = pltpu.roll(row_ref[...], shift, 1)[0:1, :]
            mine = (lane >= plan.starts[l]) & (lane < plan.starts[l] + plan.slots[l])
            idx = jnp.where(mine, rolled - me * points, idx)
        pick = jnp.where(
            lax.broadcasted_iota(jnp.int32, (points, LANES), 0) == idx, 1.0, 0.0
        ).astype(BF16)

        for r in range(slabs):
            large[r].wait()
            rows = slice(r * slab, (r + 1) * slab)
            picked = jnp.transpose(dot(emb_ref[rows, :], pick))
            for l in range(LEVELS):
                g_refs[l][:, rows] = picked[
                    plan.starts[l] : plan.starts[l] + plan.padded[l]
                ].astype(BF16)

    def in_hbm(*args):
        return [pltpu.with_memory_space_constraint(v, pltpu.HBM) for v in args]

    *owned, emb = call(
        prep_kernel,
        [jax.ShapeDtypeStruct((p, width), BF16) for p in plan.padded] + [jax.ShapeDtypeStruct((width, points), BF16)],
        *in_hbm(skeleton, embeddings),
        hbm=(0, 1),
        scratch=[
            pltpu.VMEM(skeleton.shape, jnp.int32),
            pltpu.VMEM((8, LANES), jnp.int32),
            pltpu.SemaphoreType.DMA((1 + slabs,)),
        ],
        name="prep",
        vmem=PREP_VMEM,
    )

    def tree_kernel(order_hbm, probes_hbm, list_hbm, count_hbm, emb_ref, *rest):
        x_ref, inv_ref, hn_ref, mult_ref, order_ref, probes_ref, list_ref, count_ref, sems = rest
        me = lax.axis_index("leaf")
        small = [
            pltpu.make_async_copy(src, dst, sems.at[i])
            for i, (src, dst) in enumerate(
                (
                    (order_hbm, order_ref),
                    (probes_hbm, probes_ref),
                    (list_hbm, list_ref),
                    (count_hbm, count_ref),
                )
            )
        ]
        for copy in small:
            copy.start()
        for c in range(leaves):
            sl = slice(c * LEAF, (c + 1) * LEAF)
            hn_ref[:, sl] = half_norm_row(emb_ref[:, sl])
        for copy in small:
            copy.wait()

        near = list_ref[...]
        slots = near.shape[1]
        sub = lax.broadcasted_iota(jnp.int32, (leaves, leaves), 0)
        here = sub == lax.broadcasted_iota(jnp.int32, (leaves, leaves), 1)
        count = jnp.sum(jnp.where(here, count_ref[...], 0), axis=1, keepdims=True)
        alive = lax.broadcasted_iota(jnp.int32, (leaves, slots), 1) < count
        offset = near - (me * leaves + lax.broadcasted_iota(jnp.int32, (leaves, slots), 0))
        for o in range(reach):
            hits = jnp.where(alive & (offset == o - W), 1.0, 0.0)
            mult_ref[o * leaves : (o + 1) * leaves, :] = jnp.broadcast_to(
                jnp.sum(hits, axis=1, keepdims=True), (leaves, LANES)
            )

        order_row = order_ref[...]
        low = jnp.bitwise_and(order_row, LANES - 1)
        high = jnp.right_shift(order_row, LANES.bit_length() - 1)
        hot = jnp.where(
            lax.broadcasted_iota(jnp.int32, (LANES, points), 0) == low, 1.0, 0.0
        ).astype(BF16)
        stack = jnp.concatenate(
            [probes_ref[:, h * LANES : (h + 1) * LANES] for h in range(groups)], axis=0
        )
        for c in range(leaves):
            sl = slice(c * LEAF, (c + 1) * LEAF)
            y = dot(stack, hot[:, sl])
            x = jnp.zeros((cols, LEAF), F32)
            for h in range(groups):
                x = x + jnp.where(high[:, sl] == h, y[h * cols : (h + 1) * cols], 0.0)
            x_ref[:, sl] = x.astype(BF16)

        k = lax.broadcasted_iota(jnp.int32, (8, points), 1)
        first = lax.broadcasted_iota(jnp.int32, (8, points), 0) == 0
        digits = jnp.where(first, jnp.right_shift(k, 4), jnp.bitwise_and(k, 15)).astype(F32)
        spread = jnp.concatenate(
            [jnp.where(high == h, digits, 0.0) for h in range(groups)], axis=0
        ).astype(BF16)
        found = dot_nt(spread, hot)
        for h in range(groups):
            inv_ref[:, h * LANES : (h + 1) * LANES] = (
                found[8 * h : 8 * h + 1] * 16.0 + found[8 * h + 1 : 8 * h + 2]
            ).astype(jnp.int32)

    x_tree, inv, hn, mult = call(
        tree_kernel,
        [
            jax.ShapeDtypeStruct((cols, points), BF16),
            jax.ShapeDtypeStruct((1, points), jnp.int32),
            jax.ShapeDtypeStruct((1, points), F32),
            jax.ShapeDtypeStruct((reach * leaves, LANES), F32),
        ],
        *in_hbm(order, probes, near_list, near_count),
        emb,
        hbm=(0, 1, 2, 3),
        scratch=[
            pltpu.VMEM(order.shape, jnp.int32),
            pltpu.VMEM(probes.shape, BF16),
            pltpu.VMEM(near_list.shape, jnp.int32),
            pltpu.VMEM(near_count.shape, jnp.int32),
            pltpu.SemaphoreType.DMA((4,)),
        ],
        name="tree",
    )


    def times(mult_ref, t, o, value):
        row = mult_ref[o * leaves + t : o * leaves + t + 1, :]
        return value * jnp.concatenate([row] * (LEAF // LANES), axis=1)

    def near_kernel(rows, mult_ref, emb_ref, x_ref, hn_ref, *rest):
        near_ref = rest[-1]
        acc = [None] * leaves

        def add(j, value):
            acc[j] = value if acc[j] is None else acc[j] + value

        def make(i):
            w = min(W + 1, leaves - i)
            si, sp = slice(i * LEAF, (i + 1) * LEAF), slice(i * LEAF, (i + w) * LEAF)
            g = dot(jnp.transpose(emb_ref[:, si]), emb_ref[:, sp])
            return jnp.exp(g - (col_of(hn_ref[:, si]) + hn_ref[:, sp])).astype(BF16)

        def use(i, k):
            y = dot(x_ref[:, i * LEAF : (i + 1) * LEAF], k)
            for q in range(k.shape[1] // LEAF):
                j = i + q
                sq = slice(q * LEAF, (q + 1) * LEAF)
                add(j, times(mult_ref, j, W - q, y[:, sq]))
                if q:
                    sj = slice(j * LEAF, (j + 1) * LEAF)
                    add(i, times(mult_ref, i, W + q, dot_nt(x_ref[:, sj], k[:, sq])))

        held = None
        for i in rows:
            k = make(i)
            if held is not None:
                use(*held)
            held = (i, k)
        use(*held)
        for j in range(leaves):
            sj = slice(j * LEAF, (j + 1) * LEAF)
            if len(rest) > 1:
                add(j, rest[0][:, sj])
            near_ref[:, sj] = jnp.zeros((cols, LEAF), F32) if acc[j] is None else acc[j]

    def near_part(rows, emb, x_tree, hn, *near):
        return call(
            lambda *refs: near_kernel(rows, *refs),
            jax.ShapeDtypeStruct((cols, points), F32),
            mult,
            emb,
            x_tree,
            hn,
            *near,
            flops=60 * 2 * 256**3,
            nbytes=6 << 20,
            name="near%d" % rows[0],
        )

    def low_edge(mult_ref, emb_ref, hn_ref, src_ref, near_in, near_ref):
        acc = [jnp.zeros((cols, LEAF), F32)] * W
        for q in range(W):
            sq, sp = slice(q * LEAF, (q + 1) * LEAF), slice(0, (q + 1) * LEAF)
            es = src_ref[0:width, sq]
            g = dot(jnp.transpose(es), emb_ref[:, sp])
            k = jnp.exp(g - (col_of(half_norm_row(es)) + hn_ref[:, sp])).astype(BF16)
            y = dot(src_ref[width:, sq], k)
            for t in range(q + 1):
                acc[t] = acc[t] + times(mult_ref, t, q - t, y[:, t * LEAF : (t + 1) * LEAF])
        near_ref[:, 0:halo] = near_in[:, 0:halo] + jnp.concatenate(acc, axis=1)
        near_ref[:, halo:] = near_in[:, halo:]

    def high_edge(mult_ref, emb_ref, hn_ref, src_ref, near_in, near_ref):
        acc = [jnp.zeros((cols, LEAF), F32)] * W
        for q in range(W):
            sq, sp = slice(q * LEAF, (q + 1) * LEAF), slice((leaves - W + q) * LEAF, points)
            es = src_ref[0:width, sq]
            g = dot(jnp.transpose(es), emb_ref[:, sp])
            k = jnp.exp(g - (col_of(half_norm_row(es)) + hn_ref[:, sp])).astype(BF16)
            y = dot(src_ref[width:, sq], k)
            for i in range(W - q):
                t = leaves - W + q + i
                acc[q + i] = acc[q + i] + (
                    times(mult_ref, t, leaves + q - t + W, y[:, i * LEAF : (i + 1) * LEAF])
                )
        near_ref[:, 0:last] = near_in[:, 0:last]
        near_ref[:, last:] = near_in[:, last:] + jnp.concatenate(acc, axis=1)

    def core_kernel(mult_ref, emb_ref, hn_ref, src_ref, near_in, near_ref):
        odd = jnp.bitwise_and(lax.axis_index("leaf"), 1)
        for code, edge in ((1, low_edge), (0, high_edge)):

            @pl.when(odd == code)
            def _():
                edge(mult_ref, emb_ref, hn_ref, src_ref, near_in, near_ref)

    def core_part(emb, hn, recv_a, near):
        return call(
            core_kernel,
            jax.ShapeDtypeStruct((cols, points), F32),
            mult,
            emb,
            hn,
            recv_a,
            near,
            flops=30 * 2 * 256**3,
            nbytes=3 << 20,
            name="edge_core",
        )

    def kernel_of(es, emb_ref, hn_ref, sp):
        g = dot(jnp.transpose(es), emb_ref[:, sp])
        return jnp.exp(g - (col_of(half_norm_row(es)) + hn_ref[:, sp])).astype(BF16)

    def told(src_ref, row, value):
        at = width + cols + row
        count = src_ref[at : at + 1, 0:LANES].astype(F32)
        return value * jnp.concatenate([count] * (LEAF // LANES), axis=1)

    def leaf(q):
        return slice(q * LEAF, (q + 1) * LEAF)

    def upper(mult_ref, emb_ref, hn_ref, x_ref, src_ref, near_ref, back_ref):
        k3 = kernel_of(src_ref[0:width, leaf(1)], emb_ref, hn_ref, slice(LEAF, 3 * LEAF))
        k2 = kernel_of(src_ref[0:width, leaf(0)], emb_ref, hn_ref, leaf(1))
        y3 = dot(src_ref[width : width + cols, leaf(1)], k3)
        y2 = dot(src_ref[width : width + cols, leaf(0)], k2)
        near_ref[:, leaf(1)] += times(mult_ref, 1, 1, y3[:, leaf(0)]) + times(mult_ref, 1, 0, y2)
        near_ref[:, leaf(2)] += times(mult_ref, 2, 0, y3[:, leaf(1)])
        back_ref[:, leaf(0)] = told(src_ref, 2, dot_nt(x_ref[:, leaf(1)], k2))
        back_ref[:, leaf(1)] = told(src_ref, 0, dot_nt(x_ref[:, leaf(1)], k3[:, leaf(0)])) + told(
            src_ref, 1, dot_nt(x_ref[:, leaf(2)], k3[:, leaf(1)])
        )

    def lower(mult_ref, emb_ref, hn_ref, x_ref, src_ref, near_ref, back_ref):
        k = kernel_of(src_ref[0:width, leaf(0)], emb_ref, hn_ref, slice(last, points))
        y = dot(src_ref[width : width + cols, leaf(0)], k)
        back = jnp.zeros((cols, LEAF), F32)
        for q in range(W):
            t = leaves - W + q
            near_ref[:, leaf(t)] += times(mult_ref, t, 2 * W - q, y[:, leaf(q)])
            back = back + told(src_ref, W - 1 - q, dot_nt(x_ref[:, leaf(t)], k[:, leaf(q)]))
        back_ref[:, leaf(0)] = back
        back_ref[:, leaf(1)] = jnp.zeros((cols, LEAF), F32)

    def chip_kernel(mult_ref, emb_ref, hn_ref, x_ref, one_ref, two_ref, near_in, near_ref, back_ref):
        near_ref[...] = near_in[...]
        turn = jnp.bitwise_and(lax.axis_index("leaf"), 3)
        for code, side, src_ref in (
            (1, lower, one_ref),
            (2, upper, one_ref),
            (3, lower, two_ref),
            (0, upper, two_ref),
        ):

            @pl.when(turn == code)
            def _():
                side(mult_ref, emb_ref, hn_ref, x_ref, src_ref, near_ref, back_ref)

    def chip_part(emb, recv_b1, recv_b2, near):
        return call(
            chip_kernel,
            [
                jax.ShapeDtypeStruct((cols, points), F32),
                jax.ShapeDtypeStruct((cols, UP * LEAF), F32),
            ],
            mult,
            emb,
            hn,
            x_tree,
            recv_b1,
            recv_b2,
            near,
            name="edge_chip",
        )

    table = []
    for lev, off, row in sorted(plan.entries, key=lambda e: e[2]):
        for i in range(plan.slots[lev]):
            side = (off >> plan.shift[lev]) & 1
            table.append(
                (
                    off,
                    (side * LEVELS + lev) * R + i,
                    (1 << plan.shift[lev]) - 1,
                    plan.slots[lev],
                )
            )
    table = jnp.array(table, jnp.int32).T
    own_w = LEVELS * R
    dest = table[1] + jnp.bitwise_and(pos ^ table[0], table[2]) * table[3]
    dest = dest[None, :]

    def join(*blocks):
        rows = sum(used for _, used in blocks)
        whole = all(used % 8 == 0 for _, used in blocks)
        pad = -rows % 8

        def join_kernel(*refs):
            if whole:
                row = 0
                for ref, (_, used) in zip(refs, blocks):
                    refs[-1][row : row + used, :] = ref[0:used, :]
                    row += used
            else:
                values = [ref[...].astype(F32)[0:used] for ref, (_, used) in zip(refs, blocks)]
                if pad:
                    values.append(jnp.zeros((pad, width), F32))
                refs[-1][...] = jnp.concatenate(values, axis=0).astype(BF16)

        return call(
            join_kernel,
            jax.ShapeDtypeStruct((rows + pad, width), BF16),
            *[v for v, _ in blocks],
            name="join",
        )

    after = lax.optimization_barrier
    block, used = owned[0], plan.slots[0]
    for bit in reversed(range(plan.bits)):
        level = plan.bits - bit
        stage = level - 1
        partner = lax.ppermute(block, "leaf", [(i, i ^ (1 << bit)) for i in range(n)])
        if stage == 0:
            partner, x_tree, dest = after((partner, x_tree, dest))
        if stage == 1:
            near = near_part((0, 1), emb, x_tree, hn)
            send_a = cut_core(emb, x_tree)
            partner, near, send_a = after((partner, near, send_a))
        if stage == 2:
            recv_a = lax.ppermute(send_a, "leaf", pairs_a)
            near = near_part((2, 3), emb, x_tree, hn, near)
            partner, near = after((partner, near))
        if stage == 3:
            near = near_part(tuple(range(4, leaves)), emb, x_tree, hn, near)
            emb, near = after((emb, near))
            recv_b2 = lax.ppermute(cut_chip(emb, x_tree), "leaf", pairs(3))
            near = core_part(emb, hn, recv_a, near)
            partner, near = after((partner, near))
        if bit:
            more = [(owned[level], plan.slots[level])] if level < LEVELS else []
            block = join((block, used), (partner, used), *more)
            used = 2 * used + sum(slots for _, slots in more)
            block, x_tree, emb = after((block, x_tree, emb))
    half = plan.size // 2

    def sorted_rows(first, dest_ref, *refs):
        at = lax.broadcasted_iota(jnp.int32, (own_w, half), 0)
        total = None
        for i, ref in enumerate(refs):
            d = dest_ref[:, i * half : (i + 1) * half] - first
            term = dot(jnp.where(at == d, 1.0, 0.0).astype(BF16), ref[...])
            total = term if total is None else total + term
        return total.astype(BF16)

    def own_kernel(block_ref, other_ref, dest_ref, emb_ref, x_ref, hn_ref, z_ref):
        sk = sorted_rows(0, dest_ref, block_ref, other_ref)
        hs = half_norm_col(sk)
        z = jnp.zeros((cols, own_w), F32)
        held = None
        for c in range(0, leaves, 2):
            sl = slice(c * LEAF, (c + 2) * LEAF)
            k = jnp.exp(dot(sk, emb_ref[:, sl]) - (hs + hn_ref[:, sl])).astype(BF16)
            if held is not None:
                z = z + dot_nt(x_ref[:, held[0]], held[1])
            held = (sl, k)
        z_ref[...] = z + dot_nt(x_ref[:, held[0]], held[1])

    z = call(
        own_kernel,
        jax.ShapeDtypeStruct((cols, own_w), F32),
        block,
        partner,
        dest,
        emb,
        x_tree,
        hn,
        flops=50 * 2 * 256**3,
        nbytes=4 << 20,
        name="own",
        cost=2_000_000_000,
    )

    def far_kernel(block_ref, other_ref, dest_ref, emb_ref, hn_ref, out_ref):
        sk = sorted_rows(own_w, dest_ref, block_ref, other_ref)
        hs = half_norm_col(sk)
        for c in range(0, leaves, 2):
            sl = slice(c * LEAF, (c + 2) * LEAF)
            g = dot(sk, emb_ref[:, sl])
            out_ref[:, sl] = jnp.exp(g - (hs + hn_ref[:, sl])).astype(BF16)

    def far_part(block, partner, emb, hn):
        return call(
            far_kernel,
            jax.ShapeDtypeStruct((own_w, points), BF16),
            block,
            partner,
            dest,
            emb,
            hn,
            flops=30 * 2 * 256**3,
            nbytes=4 << 20,
            name="far",
        )

    level_of = lax.broadcasted_iota(jnp.int32, (1, own_w), 1) // R
    for stage, bit in enumerate([0] + list(range(3, plan.bits)) + [2, 1]):
        heard = lax.ppermute(z, "leaf", [(i, i ^ (1 << bit)) for i in range(n)])
        if stage == 0:
            far_k = far_part(block, partner, emb, hn)
            heard, far_k, recv_b2 = after((heard, far_k, recv_b2))
        if stage == 0:
            recv_b1 = lax.ppermute(cut_chip(emb, x_tree), "leaf", pairs(1))
        if stage == 3:
            near, back = chip_part(emb, recv_b1, recv_b2, near)
            heard, near, back = after((heard, near, back))
        if stage == 4:
            back = lax.ppermute(back, "leaf", pairs(1, 3))
        swap = level_of == plan.bits - 1 - bit
        add = level_of < plan.bits - 1 - bit
        z = jnp.where(add, z + heard, jnp.where(swap, heard, z))
        z, emb = after((z, emb))

    def last_kernel(z_ref, core_ref, far_ref, back_ref, inv_ref, near_ref, out_ref):
        me = lax.axis_index("leaf")
        weights = []
        for l in range(LEVELS):
            node = 2 ** (l + 1) - 2 + (jnp.right_shift(me, plan.shift[l]) ^ 1)
            weights.append(
                jnp.dot(
                    z_ref[:, l * R : (l + 1) * R],
                    core_ref[node],
                    precision=lax.Precision.HIGHEST,
                    preferred_element_type=F32,
                ).astype(BF16)
            )
        w = jnp.concatenate(weights, axis=1)
        tree = near_ref[...] + dot(w, far_ref[...])
        even = jnp.bitwise_and(me, 1) == 0
        low_back = jnp.where(even, back_ref[:, 0:LEAF], 0.0)
        high_back = jnp.where(even, 0.0, back_ref[...])
        tree = tree + jnp.concatenate(
            [low_back, jnp.zeros((cols, points - (1 + UP) * LEAF), F32), high_back], axis=1
        )
        top = tree.astype(BF16)
        rest = (tree - top.astype(F32)).astype(BF16)
        stack = jnp.concatenate(
            [
                jnp.concatenate([v[:, h * LANES : (h + 1) * LANES] for v in (top, rest)], axis=1)
                for h in range(groups)
            ],
            axis=0,
        )
        low = jnp.bitwise_and(inv_ref[...], LANES - 1)
        high = jnp.right_shift(inv_ref[...], LANES.bit_length() - 1)
        hot = jnp.where(
            lax.broadcasted_iota(jnp.int32, (LANES, points), 0) == low, 1.0, 0.0
        ).astype(BF16)
        for c in range(leaves):
            sl = slice(c * LEAF, (c + 1) * LEAF)
            y = dot(stack, jnp.concatenate([hot[:, sl]] * 2, axis=0))
            out = jnp.zeros((cols, LEAF), F32)
            for h in range(groups):
                out = out + jnp.where(high[:, sl] == h, y[h * cols : (h + 1) * cols], 0.0)
            out_ref[:, sl] = out

    return call(
        last_kernel,
        jax.ShapeDtypeStruct((cols, points), F32),
        z,
        core,
        far_k,
        back,
        inv,
        near,
        flops=30 * 2 * 256**3,
        nbytes=2 << 20,
        name="last",
    )


def solution(mesh):
    return jax.shard_map(
        body,
        mesh=mesh,
        in_specs=(
            P(None, ("groups", "leaf")),
            P(None, ("groups", "leaf")),
            P(("groups", "leaf"), None),
            P(("groups", "leaf"), None),
            P(("groups", "leaf"), None),
            P("groups", None),
            P("groups", None, None),
        ),
        out_specs=P(None, ("groups", "leaf")),
        check_vma=False,
    )
```

```python
import jax
import jax.numpy as jnp
from jax import lax
from jax.experimental import pallas as pl
from jax.experimental.pallas import tpu as pltpu
from jax.sharding import PartitionSpec as P

LEAF = 256
R = 64
LEVELS = 4
W = 3
F32 = jnp.float32
BF16 = jnp.bfloat16
VMEM_LIMIT = 14 * 1024 * 1024
LANES = 128
PREP_VMEM = 16 * 1024 * 1024
UP = 2


def dot(a, b):
    return jnp.dot(a, b, preferred_element_type=F32)


def dot_nt(a, b):
    return lax.dot_general(a, b, (((1,), (1,)), ((), ())), preferred_element_type=F32)


def dot_tn(a, b):
    return lax.dot_general(a, b, (((0,), (0,)), ((), ())), preferred_element_type=F32)


def half_norm_row(emb):
    e = emb.astype(F32)
    return 0.5 * jnp.sum(e * e, axis=0, keepdims=True)


def half_norm_col(rows):
    e = rows.astype(F32)
    return 0.5 * jnp.sum(e * e, axis=1, keepdims=True)


def col_of(row):
    return jnp.transpose(jnp.broadcast_to(row, (8, row.shape[1])))[:, 0:1]


def call(kernel, outs, *args, scratch=(), smem=(), hbm=(), flops=0, nbytes=0, name=None, vmem=VMEM_LIMIT, cost=0):
    single = not isinstance(outs, (list, tuple))
    vm = pl.BlockSpec(memory_space=pltpu.VMEM)
    sm = pl.BlockSpec(memory_space=pltpu.SMEM)
    hb = pl.BlockSpec(memory_space=pltpu.HBM)
    return pl.pallas_call(
        kernel,
        out_shape=outs,
        in_specs=[sm if i in smem else hb if i in hbm else vm for i in range(len(args))],
        out_specs=vm if single else [vm] * len(outs),
        scratch_shapes=list(scratch),
        compiler_params=pltpu.CompilerParams(vmem_limit_bytes=vmem),
        cost_estimate=pl.CostEstimate(flops=cost, bytes_accessed=0, transcendentals=0),
        name=name,
    )(*args)


class Plan:
    def __init__(self, n):
        self.n = n
        self.bits = n.bit_length() - 1
        self.slots = [R * 2 ** (l + 1) // n for l in range(LEVELS)]
        self.padded = [-(-s // 8) * 8 for s in self.slots]
        self.starts = [sum(self.padded[:l]) for l in range(LEVELS)]
        self.rows = sum(self.padded)
        self.shift = [self.bits - 1 - l for l in range(LEVELS)]
        entries, size = [], 0
        for bit in reversed(range(self.bits)):
            level = self.bits - 1 - bit
            if level < LEVELS:
                entries.append((level, 0, size))
                size += self.slots[level]
            entries += [(lev, off ^ (1 << bit), row + size) for lev, off, row in entries]
            size *= 2
        self.entries, self.size = entries, size


def body(embeddings, probes, order, near_list, near_count, skeleton, core):
    n = lax.axis_size("leaf")
    plan = Plan(n)
    pos = lax.axis_index("leaf")
    width, points = embeddings.shape
    cols = probes.shape[0]
    leaves = points // LEAF
    halo = W * LEAF

    groups = points // LANES
    last = points - halo
    extra = 8
    slabs = 4
    slab = width // slabs
    reach = 2 * W + 1

    pairs_a = [(i, i ^ 1) for i in range(n)]

    def pairs(*starts):
        up = [(i, i + 1) for at in starts for i in range(at, n - 1, 4)]
        return up + [(j, i) for i, j in up]

    def cut_kernel(emb_ref, x_ref, a_ref, sem):
        odd = jnp.bitwise_and(lax.axis_index("leaf"), 1)
        at = pl.multiple_of((1 - odd) * last, LEAF)
        copy = pltpu.make_async_copy(
            emb_ref.at[:, pl.ds(at, halo)], a_ref.at[pl.ds(0, width), :], sem.at[0]
        )
        copy.start()
        ends = jnp.where(odd == 1, x_ref[:, :halo].astype(F32), x_ref[:, last:].astype(F32))
        a_ref[width:, :] = ends.astype(BF16)
        copy.wait()

    def cut_core(emb, x_tree):
        return call(
            cut_kernel,
            jax.ShapeDtypeStruct((width + cols, halo), BF16),
            emb,
            x_tree,
            scratch=[pltpu.SemaphoreType.DMA((1,))],
            name="cut",
        )

    def fill(b_ref, x_ref, mult_ref):
        odd = jnp.bitwise_and(lax.axis_index("leaf"), 1)

        def tell(pairs):
            rows = [mult_ref[(o + W) * leaves + t : (o + W) * leaves + t + 1, :] for t, o in pairs]
            rows.append(jnp.zeros((extra - len(rows), LANES), F32))
            b_ref[width + cols :, 0:LANES] = jnp.concatenate(rows, axis=0).astype(BF16)
            b_ref[width + cols :, LANES:] = jnp.zeros((extra, UP * LEAF - LANES), BF16)

        @pl.when(odd == 0)
        def _():
            b_ref[width : width + cols, :] = x_ref[:, : UP * LEAF]
            tell([(0, -1 - q) for q in range(W)])

        @pl.when(odd == 1)
        def _():
            b_ref[width : width + cols, :] = x_ref[:, points - UP * LEAF :]
            tell([(leaves - 1, 2), (leaves - 1, 3), (leaves - 2, 3)])

    def cut_chip_kernel(emb_ref, x_ref, mult_ref, b_ref, sem):
        odd = jnp.bitwise_and(lax.axis_index("leaf"), 1)
        at = pl.multiple_of(odd * (points - UP * LEAF), LEAF)
        copy = pltpu.make_async_copy(
            emb_ref.at[:, pl.ds(at, UP * LEAF)], b_ref.at[pl.ds(0, width), :], sem.at[0]
        )
        copy.start()
        fill(b_ref, x_ref, mult_ref)
        copy.wait()

    def cut_chip(emb, x_tree):
        return call(
            cut_chip_kernel,
            jax.ShapeDtypeStruct((width + cols + extra, UP * LEAF), BF16),
            emb,
            x_tree,
            mult,
            scratch=[pltpu.SemaphoreType.DMA((1,))],
            name="cut_chip",
        )

    def prep_kernel(skel_hbm, emb_hbm, *rest):
        g_refs, (emb_ref, skel_ref, row_ref, sems) = rest[:LEVELS], rest[LEVELS:]
        me = lax.axis_index("leaf")
        small = pltpu.make_async_copy(skel_hbm, skel_ref, sems.at[slabs])
        large = [
            pltpu.make_async_copy(
                emb_hbm.at[pl.ds(r * slab, slab), :], emb_ref.at[pl.ds(r * slab, slab), :], sems.at[r]
            )
            for r in range(slabs)
        ]
        for copy in [small] + large:
            copy.start()
        small.wait()

        lane = lax.broadcasted_iota(jnp.int32, (1, LANES), 1)
        idx = jnp.full((1, LANES), -1, jnp.int32)
        row_ref[...] = jnp.zeros_like(row_ref)
        for l in range(LEVELS):
            node = 2 ** (l + 1) - 2 + jnp.right_shift(me, plan.shift[l])
            row_ref[0:1, 0:R] = skel_ref[pl.ds(node, 1), :]
            within = jnp.bitwise_and(me, (1 << plan.shift[l]) - 1)
            shift = jnp.bitwise_and(plan.starts[l] - within * plan.slots[l] + LANES, LANES - 1)
            rolled = pltpu.roll(row_ref[...], shift, 1)[0:1, :]
            mine = (lane >= plan.starts[l]) & (lane < plan.starts[l] + plan.slots[l])
            idx = jnp.where(mine, rolled - me * points, idx)
        pick = jnp.where(
            lax.broadcasted_iota(jnp.int32, (points, LANES), 0) == idx, 1.0, 0.0
        ).astype(BF16)

        for r in range(slabs):
            large[r].wait()
            rows = slice(r * slab, (r + 1) * slab)
            picked = jnp.transpose(dot(emb_ref[rows, :], pick))
            for l in range(LEVELS):
                g_refs[l][:, rows] = picked[
                    plan.starts[l] : plan.starts[l] + plan.padded[l]
                ].astype(BF16)

    def in_hbm(*args):
        return [pltpu.with_memory_space_constraint(v, pltpu.HBM) for v in args]

    *owned, emb = call(
        prep_kernel,
        [jax.ShapeDtypeStruct((p, width), BF16) for p in plan.padded] + [jax.ShapeDtypeStruct((width, points), BF16)],
        *in_hbm(skeleton, embeddings),
        hbm=(0, 1),
        scratch=[
            pltpu.VMEM(skeleton.shape, jnp.int32),
            pltpu.VMEM((8, LANES), jnp.int32),
            pltpu.SemaphoreType.DMA((1 + slabs,)),
        ],
        name="prep",
        vmem=PREP_VMEM,
    )

    def tree_kernel(order_hbm, probes_hbm, list_hbm, count_hbm, emb_ref, *rest):
        x_ref, inv_ref, hn_ref, mult_ref, order_ref, probes_ref, list_ref, count_ref, sems = rest
        me = lax.axis_index("leaf")
        small = [
            pltpu.make_async_copy(src, dst, sems.at[i])
            for i, (src, dst) in enumerate(
                (
                    (order_hbm, order_ref),
                    (probes_hbm, probes_ref),
                    (list_hbm, list_ref),
                    (count_hbm, count_ref),
                )
            )
        ]
        for copy in small:
            copy.start()
        for c in range(leaves):
            sl = slice(c * LEAF, (c + 1) * LEAF)
            hn_ref[:, sl] = half_norm_row(emb_ref[:, sl])
        for copy in small:
            copy.wait()

        near = list_ref[...]
        slots = near.shape[1]
        sub = lax.broadcasted_iota(jnp.int32, (leaves, leaves), 0)
        here = sub == lax.broadcasted_iota(jnp.int32, (leaves, leaves), 1)
        count = jnp.sum(jnp.where(here, count_ref[...], 0), axis=1, keepdims=True)
        alive = lax.broadcasted_iota(jnp.int32, (leaves, slots), 1) < count
        offset = near - (me * leaves + lax.broadcasted_iota(jnp.int32, (leaves, slots), 0))
        for o in range(reach):
            hits = jnp.where(alive & (offset == o - W), 1.0, 0.0)
            mult_ref[o * leaves : (o + 1) * leaves, :] = jnp.broadcast_to(
                jnp.sum(hits, axis=1, keepdims=True), (leaves, LANES)
            )

        order_row = order_ref[...]
        low = jnp.bitwise_and(order_row, LANES - 1)
        high = jnp.right_shift(order_row, LANES.bit_length() - 1)
        hot = jnp.where(
            lax.broadcasted_iota(jnp.int32, (LANES, points), 0) == low, 1.0, 0.0
        ).astype(BF16)
        stack = jnp.concatenate(
            [probes_ref[:, h * LANES : (h + 1) * LANES] for h in range(groups)], axis=0
        )
        for c in range(leaves):
            sl = slice(c * LEAF, (c + 1) * LEAF)
            y = dot(stack, hot[:, sl])
            x = jnp.zeros((cols, LEAF), F32)
            for h in range(groups):
                x = x + jnp.where(high[:, sl] == h, y[h * cols : (h + 1) * cols], 0.0)
            x_ref[:, sl] = x.astype(BF16)

        k = lax.broadcasted_iota(jnp.int32, (8, points), 1)
        first = lax.broadcasted_iota(jnp.int32, (8, points), 0) == 0
        digits = jnp.where(first, jnp.right_shift(k, 4), jnp.bitwise_and(k, 15)).astype(F32)
        spread = jnp.concatenate(
            [jnp.where(high == h, digits, 0.0) for h in range(groups)], axis=0
        ).astype(BF16)
        found = dot_nt(spread, hot)
        for h in range(groups):
            inv_ref[:, h * LANES : (h + 1) * LANES] = (
                found[8 * h : 8 * h + 1] * 16.0 + found[8 * h + 1 : 8 * h + 2]
            ).astype(jnp.int32)

    x_tree, inv, hn, mult = call(
        tree_kernel,
        [
            jax.ShapeDtypeStruct((cols, points), BF16),
            jax.ShapeDtypeStruct((1, points), jnp.int32),
            jax.ShapeDtypeStruct((1, points), F32),
            jax.ShapeDtypeStruct((reach * leaves, LANES), F32),
        ],
        *in_hbm(order, probes, near_list, near_count),
        emb,
        hbm=(0, 1, 2, 3),
        scratch=[
            pltpu.VMEM(order.shape, jnp.int32),
            pltpu.VMEM(probes.shape, BF16),
            pltpu.VMEM(near_list.shape, jnp.int32),
            pltpu.VMEM(near_count.shape, jnp.int32),
            pltpu.SemaphoreType.DMA((4,)),
        ],
        name="tree",
    )


    def times(mult_ref, t, o, value):
        row = mult_ref[o * leaves + t : o * leaves + t + 1, :]
        return value * jnp.concatenate([row] * (LEAF // LANES), axis=1)

    def near_kernel(rows, mult_ref, emb_ref, x_ref, hn_ref, *rest):
        near_ref = rest[-1]
        acc = [None] * leaves

        def add(j, value):
            acc[j] = value if acc[j] is None else acc[j] + value

        def make(i):
            w = min(W + 1, leaves - i)
            si, sp = slice(i * LEAF, (i + 1) * LEAF), slice(i * LEAF, (i + w) * LEAF)
            g = dot(jnp.transpose(emb_ref[:, si]), emb_ref[:, sp])
            return jnp.exp(g - (col_of(hn_ref[:, si]) + hn_ref[:, sp])).astype(BF16)

        def use(i, k):
            y = dot(x_ref[:, i * LEAF : (i + 1) * LEAF], k)
            for q in range(k.shape[1] // LEAF):
                j = i + q
                sq = slice(q * LEAF, (q + 1) * LEAF)
                add(j, times(mult_ref, j, W - q, y[:, sq]))
                if q:
                    sj = slice(j * LEAF, (j + 1) * LEAF)
                    add(i, times(mult_ref, i, W + q, dot_nt(x_ref[:, sj], k[:, sq])))

        held = None
        for i in rows:
            k = make(i)
            if held is not None:
                use(*held)
            held = (i, k)
        use(*held)
        for j in range(leaves):
            sj = slice(j * LEAF, (j + 1) * LEAF)
            if len(rest) > 1:
                add(j, rest[0][:, sj])
            near_ref[:, sj] = jnp.zeros((cols, LEAF), F32) if acc[j] is None else acc[j]

    def near_part(rows, emb, x_tree, hn, *near):
        return call(
            lambda *refs: near_kernel(rows, *refs),
            jax.ShapeDtypeStruct((cols, points), F32),
            mult,
            emb,
            x_tree,
            hn,
            *near,
            flops=60 * 2 * 256**3,
            nbytes=6 << 20,
            name="near%d" % rows[0],
        )

    def low_edge(mult_ref, emb_ref, hn_ref, src_ref, near_in, near_ref):
        acc = [jnp.zeros((cols, LEAF), F32)] * W
        for q in range(W):
            sq, sp = slice(q * LEAF, (q + 1) * LEAF), slice(0, (q + 1) * LEAF)
            es = src_ref[0:width, sq]
            g = dot(jnp.transpose(es), emb_ref[:, sp])
            k = jnp.exp(g - (col_of(half_norm_row(es)) + hn_ref[:, sp])).astype(BF16)
            y = dot(src_ref[width:, sq], k)
            for t in range(q + 1):
                acc[t] = acc[t] + times(mult_ref, t, q - t, y[:, t * LEAF : (t + 1) * LEAF])
        near_ref[:, 0:halo] = near_in[:, 0:halo] + jnp.concatenate(acc, axis=1)
        near_ref[:, halo:] = near_in[:, halo:]

    def high_edge(mult_ref, emb_ref, hn_ref, src_ref, near_in, near_ref):
        acc = [jnp.zeros((cols, LEAF), F32)] * W
        for q in range(W):
            sq, sp = slice(q * LEAF, (q + 1) * LEAF), slice((leaves - W + q) * LEAF, points)
            es = src_ref[0:width, sq]
            g = dot(jnp.transpose(es), emb_ref[:, sp])
            k = jnp.exp(g - (col_of(half_norm_row(es)) + hn_ref[:, sp])).astype(BF16)
            y = dot(src_ref[width:, sq], k)
            for i in range(W - q):
                t = leaves - W + q + i
                acc[q + i] = acc[q + i] + (
                    times(mult_ref, t, leaves + q - t + W, y[:, i * LEAF : (i + 1) * LEAF])
                )
        near_ref[:, 0:last] = near_in[:, 0:last]
        near_ref[:, last:] = near_in[:, last:] + jnp.concatenate(acc, axis=1)

    def core_kernel(mult_ref, emb_ref, hn_ref, src_ref, near_in, near_ref):
        odd = jnp.bitwise_and(lax.axis_index("leaf"), 1)
        for code, edge in ((1, low_edge), (0, high_edge)):

            @pl.when(odd == code)
            def _():
                edge(mult_ref, emb_ref, hn_ref, src_ref, near_in, near_ref)

    def core_part(emb, hn, recv_a, near):
        return call(
            core_kernel,
            jax.ShapeDtypeStruct((cols, points), F32),
            mult,
            emb,
            hn,
            recv_a,
            near,
            flops=30 * 2 * 256**3,
            nbytes=3 << 20,
            name="edge_core",
        )

    def kernel_of(es, emb_ref, hn_ref, sp):
        g = dot(jnp.transpose(es), emb_ref[:, sp])
        return jnp.exp(g - (col_of(half_norm_row(es)) + hn_ref[:, sp])).astype(BF16)

    def told(src_ref, row, value):
        at = width + cols + row
        count = src_ref[at : at + 1, 0:LANES].astype(F32)
        return value * jnp.concatenate([count] * (LEAF // LANES), axis=1)

    def leaf(q):
        return slice(q * LEAF, (q + 1) * LEAF)

    def upper(mult_ref, emb_ref, hn_ref, x_ref, src_ref, near_ref, back_ref):
        k3 = kernel_of(src_ref[0:width, leaf(1)], emb_ref, hn_ref, slice(LEAF, 3 * LEAF))
        k2 = kernel_of(src_ref[0:width, leaf(0)], emb_ref, hn_ref, leaf(1))
        y3 = dot(src_ref[width : width + cols, leaf(1)], k3)
        y2 = dot(src_ref[width : width + cols, leaf(0)], k2)
        near_ref[:, leaf(1)] += times(mult_ref, 1, 1, y3[:, leaf(0)]) + times(mult_ref, 1, 0, y2)
        near_ref[:, leaf(2)] += times(mult_ref, 2, 0, y3[:, leaf(1)])
        back_ref[:, leaf(0)] = told(src_ref, 2, dot_nt(x_ref[:, leaf(1)], k2))
        back_ref[:, leaf(1)] = told(src_ref, 0, dot_nt(x_ref[:, leaf(1)], k3[:, leaf(0)])) + told(
            src_ref, 1, dot_nt(x_ref[:, leaf(2)], k3[:, leaf(1)])
        )

    def lower(mult_ref, emb_ref, hn_ref, x_ref, src_ref, near_ref, back_ref):
        k = kernel_of(src_ref[0:width, leaf(0)], emb_ref, hn_ref, slice(last, points))
        y = dot(src_ref[width : width + cols, leaf(0)], k)
        back = jnp.zeros((cols, LEAF), F32)
        for q in range(W):
            t = leaves - W + q
            near_ref[:, leaf(t)] += times(mult_ref, t, 2 * W - q, y[:, leaf(q)])
            back = back + told(src_ref, W - 1 - q, dot_nt(x_ref[:, leaf(t)], k[:, leaf(q)]))
        back_ref[:, leaf(0)] = back
        back_ref[:, leaf(1)] = jnp.zeros((cols, LEAF), F32)

    def chip_kernel(mult_ref, emb_ref, hn_ref, x_ref, one_ref, two_ref, near_in, near_ref, back_ref):
        near_ref[...] = near_in[...]
        turn = jnp.bitwise_and(lax.axis_index("leaf"), 3)
        for code, side, src_ref in (
            (1, lower, one_ref),
            (2, upper, one_ref),
            (3, lower, two_ref),
            (0, upper, two_ref),
        ):

            @pl.when(turn == code)
            def _():
                side(mult_ref, emb_ref, hn_ref, x_ref, src_ref, near_ref, back_ref)

    def chip_part(emb, recv_b1, recv_b2, near):
        return call(
            chip_kernel,
            [
                jax.ShapeDtypeStruct((cols, points), F32),
                jax.ShapeDtypeStruct((cols, UP * LEAF), F32),
            ],
            mult,
            emb,
            hn,
            x_tree,
            recv_b1,
            recv_b2,
            near,
            name="edge_chip",
        )

    table = []
    for lev, off, row in sorted(plan.entries, key=lambda e: e[2]):
        for i in range(plan.slots[lev]):
            side = (off >> plan.shift[lev]) & 1
            table.append(
                (
                    off,
                    (side * LEVELS + lev) * R + i,
                    (1 << plan.shift[lev]) - 1,
                    plan.slots[lev],
                )
            )
    table = jnp.array(table, jnp.int32).T
    own_w = LEVELS * R
    dest = table[1] + jnp.bitwise_and(pos ^ table[0], table[2]) * table[3]
    dest = dest[None, :]

    def join(*blocks):
        rows = sum(used for _, used in blocks)
        whole = all(used % 8 == 0 for _, used in blocks)
        pad = -rows % 8

        def join_kernel(*refs):
            if whole:
                row = 0
                for ref, (_, used) in zip(refs, blocks):
                    refs[-1][row : row + used, :] = ref[0:used, :]
                    row += used
            else:
                values = [ref[...].astype(F32)[0:used] for ref, (_, used) in zip(refs, blocks)]
                if pad:
                    values.append(jnp.zeros((pad, width), F32))
                refs[-1][...] = jnp.concatenate(values, axis=0).astype(BF16)

        return call(
            join_kernel,
            jax.ShapeDtypeStruct((rows + pad, width), BF16),
            *[v for v, _ in blocks],
            name="join",
        )

    after = lax.optimization_barrier
    block, used = owned[0], plan.slots[0]
    for bit in reversed(range(plan.bits)):
        level = plan.bits - bit
        stage = level - 1
        partner = lax.ppermute(block, "leaf", [(i, i ^ (1 << bit)) for i in range(n)])
        if stage == 0:
            partner, x_tree, dest = after((partner, x_tree, dest))
        if stage == 1:
            near = near_part((0, 1), emb, x_tree, hn)
            send_a = cut_core(emb, x_tree)
            partner, near, send_a = after((partner, near, send_a))
        if stage == 2:
            recv_a = lax.ppermute(send_a, "leaf", pairs_a)
            near = near_part((2, 3), emb, x_tree, hn, near)
            partner, near = after((partner, near))
        if stage == 3:
            near = near_part(tuple(range(4, leaves)), emb, x_tree, hn, near)
            recv_b2 = lax.ppermute(cut_chip(emb, x_tree), "leaf", pairs(3))
            near = core_part(emb, hn, recv_a, near)
            partner, near = after((partner, near))
        if bit:
            more = [(owned[level], plan.slots[level])] if level < LEVELS else []
            block = join((block, used), (partner, used), *more)
            used = 2 * used + sum(slots for _, slots in more)
            block, x_tree, emb = after((block, x_tree, emb))
    half = plan.size // 2

    def sorted_rows(first, dest_ref, *refs):
        at = lax.broadcasted_iota(jnp.int32, (own_w, half), 0)
        total = None
        for i, ref in enumerate(refs):
            d = dest_ref[:, i * half : (i + 1) * half] - first
            term = dot(jnp.where(at == d, 1.0, 0.0).astype(BF16), ref[...])
            total = term if total is None else total + term
        return total.astype(BF16)

    def own_kernel(block_ref, other_ref, dest_ref, emb_ref, x_ref, hn_ref, z_ref):
        sk = sorted_rows(0, dest_ref, block_ref, other_ref)
        hs = half_norm_col(sk)
        z = jnp.zeros((cols, own_w), F32)
        held = None
        for c in range(0, leaves, 2):
            sl = slice(c * LEAF, (c + 2) * LEAF)
            k = jnp.exp(dot(sk, emb_ref[:, sl]) - (hs + hn_ref[:, sl])).astype(BF16)
            if held is not None:
                z = z + dot_nt(x_ref[:, held[0]], held[1])
            held = (sl, k)
        z_ref[...] = z + dot_nt(x_ref[:, held[0]], held[1])

    z = call(
        own_kernel,
        jax.ShapeDtypeStruct((cols, own_w), F32),
        block,
        partner,
        dest,
        emb,
        x_tree,
        hn,
        flops=50 * 2 * 256**3,
        nbytes=4 << 20,
        name="own",
        cost=3_000_000_000,
    )

    def far_kernel(block_ref, other_ref, dest_ref, emb_ref, hn_ref, out_ref):
        sk = sorted_rows(own_w, dest_ref, block_ref, other_ref)
        hs = half_norm_col(sk)
        for c in range(0, leaves, 2):
            sl = slice(c * LEAF, (c + 2) * LEAF)
            g = dot(sk, emb_ref[:, sl])
            out_ref[:, sl] = jnp.exp(g - (hs + hn_ref[:, sl])).astype(BF16)

    def far_part(block, partner, emb, hn):
        return call(
            far_kernel,
            jax.ShapeDtypeStruct((own_w, points), BF16),
            block,
            partner,
            dest,
            emb,
            hn,
            flops=30 * 2 * 256**3,
            nbytes=4 << 20,
            name="far",
        )

    level_of = lax.broadcasted_iota(jnp.int32, (1, own_w), 1) // R
    for stage, bit in enumerate([0] + list(range(3, plan.bits)) + [2, 1]):
        heard = lax.ppermute(z, "leaf", [(i, i ^ (1 << bit)) for i in range(n)])
        if stage == 0:
            far_k = far_part(block, partner, emb, hn)
            heard, far_k, recv_b2 = after((heard, far_k, recv_b2))
        if stage == 0:
            recv_b1 = lax.ppermute(cut_chip(emb, x_tree), "leaf", pairs(1))
        if stage == 3:
            near, back = chip_part(emb, recv_b1, recv_b2, near)
            heard, near, back = after((heard, near, back))
        if stage == 4:
            back = lax.ppermute(back, "leaf", pairs(1, 3))
        swap = level_of == plan.bits - 1 - bit
        add = level_of < plan.bits - 1 - bit
        z = jnp.where(add, z + heard, jnp.where(swap, heard, z))
        z, emb = after((z, emb))

    def last_kernel(z_ref, core_ref, far_ref, back_ref, inv_ref, near_ref, out_ref):
        me = lax.axis_index("leaf")
        weights = []
        for l in range(LEVELS):
            node = 2 ** (l + 1) - 2 + (jnp.right_shift(me, plan.shift[l]) ^ 1)
            weights.append(
                jnp.dot(
                    z_ref[:, l * R : (l + 1) * R],
                    core_ref[node],
                    precision=lax.Precision.HIGHEST,
                    preferred_element_type=F32,
                ).astype(BF16)
            )
        w = jnp.concatenate(weights, axis=1)
        tree = near_ref[...] + dot(w, far_ref[...])
        even = jnp.bitwise_and(me, 1) == 0
        low_back = jnp.where(even, back_ref[:, 0:LEAF], 0.0)
        high_back = jnp.where(even, 0.0, back_ref[...])
        tree = tree + jnp.concatenate(
            [low_back, jnp.zeros((cols, points - (1 + UP) * LEAF), F32), high_back], axis=1
        )
        top = tree.astype(BF16)
        rest = (tree - top.astype(F32)).astype(BF16)
        stack = jnp.concatenate(
            [
                jnp.concatenate([v[:, h * LANES : (h + 1) * LANES] for v in (top, rest)], axis=1)
                for h in range(groups)
            ],
            axis=0,
        )
        low = jnp.bitwise_and(inv_ref[...], LANES - 1)
        high = jnp.right_shift(inv_ref[...], LANES.bit_length() - 1)
        hot = jnp.where(
            lax.broadcasted_iota(jnp.int32, (LANES, points), 0) == low, 1.0, 0.0
        ).astype(BF16)
        for c in range(leaves):
            sl = slice(c * LEAF, (c + 1) * LEAF)
            y = dot(stack, jnp.concatenate([hot[:, sl]] * 2, axis=0))
            out = jnp.zeros((cols, LEAF), F32)
            for h in range(groups):
                out = out + jnp.where(high[:, sl] == h, y[h * cols : (h + 1) * cols], 0.0)
            out_ref[:, sl] = out

    return call(
        last_kernel,
        jax.ShapeDtypeStruct((cols, points), F32),
        z,
        core,
        far_k,
        back,
        inv,
        near,
        flops=30 * 2 * 256**3,
        nbytes=2 << 20,
        name="last",
    )


def solution(mesh):
    return jax.shard_map(
        body,
        mesh=mesh,
        in_specs=(
            P(None, ("groups", "leaf")),
            P(None, ("groups", "leaf")),
            P(("groups", "leaf"), None),
            P(("groups", "leaf"), None),
            P(("groups", "leaf"), None),
            P("groups", None),
            P("groups", None, None),
        ),
        out_specs=P(None, ("groups", "leaf")),
        check_vma=False,
    )
```

```python
import jax
import jax.numpy as jnp
from jax import lax
from jax.experimental import pallas as pl
from jax.experimental.pallas import tpu as pltpu
from jax.sharding import PartitionSpec as P

LEAF = 256
R = 64
LEVELS = 4
W = 3
F32 = jnp.float32
BF16 = jnp.bfloat16
VMEM_LIMIT = 14 * 1024 * 1024
LANES = 128
PREP_VMEM = 16 * 1024 * 1024
UP = 2


def dot(a, b):
    return jnp.dot(a, b, preferred_element_type=F32)


def dot_nt(a, b):
    return lax.dot_general(a, b, (((1,), (1,)), ((), ())), preferred_element_type=F32)


def dot_tn(a, b):
    return lax.dot_general(a, b, (((0,), (0,)), ((), ())), preferred_element_type=F32)


def half_norm_row(emb):
    e = emb.astype(F32)
    return 0.5 * jnp.sum(e * e, axis=0, keepdims=True)


def half_norm_col(rows):
    e = rows.astype(F32)
    return 0.5 * jnp.sum(e * e, axis=1, keepdims=True)


def col_of(row):
    return jnp.transpose(jnp.broadcast_to(row, (8, row.shape[1])))[:, 0:1]


def call(kernel, outs, *args, scratch=(), smem=(), hbm=(), flops=0, nbytes=0, name=None, vmem=VMEM_LIMIT, cost=0):
    single = not isinstance(outs, (list, tuple))
    vm = pl.BlockSpec(memory_space=pltpu.VMEM)
    sm = pl.BlockSpec(memory_space=pltpu.SMEM)
    hb = pl.BlockSpec(memory_space=pltpu.HBM)
    return pl.pallas_call(
        kernel,
        out_shape=outs,
        in_specs=[sm if i in smem else hb if i in hbm else vm for i in range(len(args))],
        out_specs=vm if single else [vm] * len(outs),
        scratch_shapes=list(scratch),
        compiler_params=pltpu.CompilerParams(vmem_limit_bytes=vmem),
        cost_estimate=pl.CostEstimate(flops=cost, bytes_accessed=0, transcendentals=0),
        name=name,
    )(*args)


class Plan:
    def __init__(self, n):
        self.n = n
        self.bits = n.bit_length() - 1
        self.slots = [R * 2 ** (l + 1) // n for l in range(LEVELS)]
        self.padded = [-(-s // 8) * 8 for s in self.slots]
        self.starts = [sum(self.padded[:l]) for l in range(LEVELS)]
        self.rows = sum(self.padded)
        self.shift = [self.bits - 1 - l for l in range(LEVELS)]
        entries, size = [], 0
        for bit in reversed(range(self.bits)):
            level = self.bits - 1 - bit
            if level < LEVELS:
                entries.append((level, 0, size))
                size += self.slots[level]
            entries += [(lev, off ^ (1 << bit), row + size) for lev, off, row in entries]
            size *= 2
        self.entries, self.size = entries, size


def body(embeddings, probes, order, near_list, near_count, skeleton, core):
    n = lax.axis_size("leaf")
    plan = Plan(n)
    pos = lax.axis_index("leaf")
    width, points = embeddings.shape
    cols = probes.shape[0]
    leaves = points // LEAF
    halo = W * LEAF

    groups = points // LANES
    last = points - halo
    extra = 8
    slabs = 4
    slab = width // slabs
    reach = 2 * W + 1

    pairs_a = [(i, i ^ 1) for i in range(n)]

    def pairs(*starts):
        up = [(i, i + 1) for at in starts for i in range(at, n - 1, 4)]
        return up + [(j, i) for i, j in up]

    def cut_kernel(emb_ref, x_ref, a_ref, sem):
        odd = jnp.bitwise_and(lax.axis_index("leaf"), 1)
        at = pl.multiple_of((1 - odd) * last, LEAF)
        copy = pltpu.make_async_copy(
            emb_ref.at[:, pl.ds(at, halo)], a_ref.at[pl.ds(0, width), :], sem.at[0]
        )
        copy.start()
        ends = jnp.where(odd == 1, x_ref[:, :halo].astype(F32), x_ref[:, last:].astype(F32))
        a_ref[width:, :] = ends.astype(BF16)
        copy.wait()

    def cut_core(emb, x_tree):
        return call(
            cut_kernel,
            jax.ShapeDtypeStruct((width + cols, halo), BF16),
            emb,
            x_tree,
            scratch=[pltpu.SemaphoreType.DMA((1,))],
            name="cut",
        )

    def fill(b_ref, x_ref, mult_ref):
        odd = jnp.bitwise_and(lax.axis_index("leaf"), 1)

        def tell(pairs):
            rows = [mult_ref[(o + W) * leaves + t : (o + W) * leaves + t + 1, :] for t, o in pairs]
            rows.append(jnp.zeros((extra - len(rows), LANES), F32))
            b_ref[width + cols :, 0:LANES] = jnp.concatenate(rows, axis=0).astype(BF16)
            b_ref[width + cols :, LANES:] = jnp.zeros((extra, UP * LEAF - LANES), BF16)

        @pl.when(odd == 0)
        def _():
            b_ref[width : width + cols, :] = x_ref[:, : UP * LEAF]
            tell([(0, -1 - q) for q in range(W)])

        @pl.when(odd == 1)
        def _():
            b_ref[width : width + cols, :] = x_ref[:, points - UP * LEAF :]
            tell([(leaves - 1, 2), (leaves - 1, 3), (leaves - 2, 3)])

    def cut_chip_kernel(emb_ref, x_ref, mult_ref, b_ref, sem):
        odd = jnp.bitwise_and(lax.axis_index("leaf"), 1)
        at = pl.multiple_of(odd * (points - UP * LEAF), LEAF)
        copy = pltpu.make_async_copy(
            emb_ref.at[:, pl.ds(at, UP * LEAF)], b_ref.at[pl.ds(0, width), :], sem.at[0]
        )
        copy.start()
        fill(b_ref, x_ref, mult_ref)
        copy.wait()

    def cut_chip(emb, x_tree):
        return call(
            cut_chip_kernel,
            jax.ShapeDtypeStruct((width + cols + extra, UP * LEAF), BF16),
            emb,
            x_tree,
            mult,
            scratch=[pltpu.SemaphoreType.DMA((1,))],
            name="cut_chip",
        )

    def prep_kernel(skel_hbm, emb_hbm, *rest):
        g_refs, (emb_ref, skel_ref, row_ref, sems) = rest[:LEVELS], rest[LEVELS:]
        me = lax.axis_index("leaf")
        small = pltpu.make_async_copy(skel_hbm, skel_ref, sems.at[slabs])
        large = [
            pltpu.make_async_copy(
                emb_hbm.at[pl.ds(r * slab, slab), :], emb_ref.at[pl.ds(r * slab, slab), :], sems.at[r]
            )
            for r in range(slabs)
        ]
        for copy in [small] + large:
            copy.start()
        small.wait()

        lane = lax.broadcasted_iota(jnp.int32, (1, LANES), 1)
        idx = jnp.full((1, LANES), -1, jnp.int32)
        row_ref[...] = jnp.zeros_like(row_ref)
        for l in range(LEVELS):
            node = 2 ** (l + 1) - 2 + jnp.right_shift(me, plan.shift[l])
            row_ref[0:1, 0:R] = skel_ref[pl.ds(node, 1), :]
            within = jnp.bitwise_and(me, (1 << plan.shift[l]) - 1)
            shift = jnp.bitwise_and(plan.starts[l] - within * plan.slots[l] + LANES, LANES - 1)
            rolled = pltpu.roll(row_ref[...], shift, 1)[0:1, :]
            mine = (lane >= plan.starts[l]) & (lane < plan.starts[l] + plan.slots[l])
            idx = jnp.where(mine, rolled - me * points, idx)
        pick = jnp.where(
            lax.broadcasted_iota(jnp.int32, (points, LANES), 0) == idx, 1.0, 0.0
        ).astype(BF16)

        for r in range(slabs):
            large[r].wait()
            rows = slice(r * slab, (r + 1) * slab)
            picked = jnp.transpose(dot(emb_ref[rows, :], pick))
            for l in range(LEVELS):
                g_refs[l][:, rows] = picked[
                    plan.starts[l] : plan.starts[l] + plan.padded[l]
                ].astype(BF16)

    def in_hbm(*args):
        return [pltpu.with_memory_space_constraint(v, pltpu.HBM) for v in args]

    *owned, emb = call(
        prep_kernel,
        [jax.ShapeDtypeStruct((p, width), BF16) for p in plan.padded] + [jax.ShapeDtypeStruct((width, points), BF16)],
        *in_hbm(skeleton, embeddings),
        hbm=(0, 1),
        scratch=[
            pltpu.VMEM(skeleton.shape, jnp.int32),
            pltpu.VMEM((8, LANES), jnp.int32),
            pltpu.SemaphoreType.DMA((1 + slabs,)),
        ],
        name="prep",
        vmem=PREP_VMEM,
    )

    def tree_kernel(order_hbm, probes_hbm, list_hbm, count_hbm, emb_ref, *rest):
        x_ref, inv_ref, hn_ref, mult_ref, order_ref, probes_ref, list_ref, count_ref, sems = rest
        me = lax.axis_index("leaf")
        small = [
            pltpu.make_async_copy(src, dst, sems.at[i])
            for i, (src, dst) in enumerate(
                (
                    (order_hbm, order_ref),
                    (probes_hbm, probes_ref),
                    (list_hbm, list_ref),
                    (count_hbm, count_ref),
                )
            )
        ]
        for copy in small:
            copy.start()
        for c in range(leaves):
            sl = slice(c * LEAF, (c + 1) * LEAF)
            hn_ref[:, sl] = half_norm_row(emb_ref[:, sl])
        for copy in small:
            copy.wait()

        near = list_ref[...]
        slots = near.shape[1]
        sub = lax.broadcasted_iota(jnp.int32, (leaves, leaves), 0)
        here = sub == lax.broadcasted_iota(jnp.int32, (leaves, leaves), 1)
        count = jnp.sum(jnp.where(here, count_ref[...], 0), axis=1, keepdims=True)
        alive = lax.broadcasted_iota(jnp.int32, (leaves, slots), 1) < count
        offset = near - (me * leaves + lax.broadcasted_iota(jnp.int32, (leaves, slots), 0))
        for o in range(reach):
            hits = jnp.where(alive & (offset == o - W), 1.0, 0.0)
            mult_ref[o * leaves : (o + 1) * leaves, :] = jnp.broadcast_to(
                jnp.sum(hits, axis=1, keepdims=True), (leaves, LANES)
            )

        order_row = order_ref[...]
        low = jnp.bitwise_and(order_row, LANES - 1)
        high = jnp.right_shift(order_row, LANES.bit_length() - 1)
        hot = jnp.where(
            lax.broadcasted_iota(jnp.int32, (LANES, points), 0) == low, 1.0, 0.0
        ).astype(BF16)
        stack = jnp.concatenate(
            [probes_ref[:, h * LANES : (h + 1) * LANES] for h in range(groups)], axis=0
        )
        for c in range(leaves):
            sl = slice(c * LEAF, (c + 1) * LEAF)
            y = dot(stack, hot[:, sl])
            x = jnp.zeros((cols, LEAF), F32)
            for h in range(groups):
                x = jnp.where(high[:, sl] == h, y[h * cols : (h + 1) * cols], x)
            x_ref[:, sl] = x.astype(BF16)

        k = lax.broadcasted_iota(jnp.int32, (8, points), 1)
        first = lax.broadcasted_iota(jnp.int32, (8, points), 0) == 0
        digits = jnp.where(first, jnp.right_shift(k, 4), jnp.bitwise_and(k, 15)).astype(F32)
        spread = jnp.concatenate(
            [jnp.where(high == h, digits, 0.0) for h in range(groups)], axis=0
        ).astype(BF16)
        found = dot_nt(spread, hot)
        for h in range(groups):
            inv_ref[:, h * LANES : (h + 1) * LANES] = (
                found[8 * h : 8 * h + 1] * 16.0 + found[8 * h + 1 : 8 * h + 2]
            ).astype(jnp.int32)

    x_tree, inv, hn, mult = call(
        tree_kernel,
        [
            jax.ShapeDtypeStruct((cols, points), BF16),
            jax.ShapeDtypeStruct((1, points), jnp.int32),
            jax.ShapeDtypeStruct((1, points), F32),
            jax.ShapeDtypeStruct((reach * leaves, LANES), F32),
        ],
        *in_hbm(order, probes, near_list, near_count),
        emb,
        hbm=(0, 1, 2, 3),
        scratch=[
            pltpu.VMEM(order.shape, jnp.int32),
            pltpu.VMEM(probes.shape, BF16),
            pltpu.VMEM(near_list.shape, jnp.int32),
            pltpu.VMEM(near_count.shape, jnp.int32),
            pltpu.SemaphoreType.DMA((4,)),
        ],
        name="tree",
    )


    def times(mult_ref, t, o, value):
        row = mult_ref[o * leaves + t : o * leaves + t + 1, :]
        return value * jnp.concatenate([row] * (LEAF // LANES), axis=1)

    def near_kernel(rows, mult_ref, emb_ref, x_ref, hn_ref, *rest):
        near_ref = rest[-1]
        acc = [None] * leaves

        def add(j, value):
            acc[j] = value if acc[j] is None else acc[j] + value

        def make(i):
            w = min(W + 1, leaves - i)
            si, sp = slice(i * LEAF, (i + 1) * LEAF), slice(i * LEAF, (i + w) * LEAF)
            g = dot(jnp.transpose(emb_ref[:, si]), emb_ref[:, sp])
            return jnp.exp(g - (col_of(hn_ref[:, si]) + hn_ref[:, sp])).astype(BF16)

        def use(i, k):
            y = dot(x_ref[:, i * LEAF : (i + 1) * LEAF], k)
            for q in range(k.shape[1] // LEAF):
                j = i + q
                sq = slice(q * LEAF, (q + 1) * LEAF)
                add(j, times(mult_ref, j, W - q, y[:, sq]))
                if q:
                    sj = slice(j * LEAF, (j + 1) * LEAF)
                    add(i, times(mult_ref, i, W + q, dot_nt(x_ref[:, sj], k[:, sq])))

        held = None
        for i in rows:
            k = make(i)
            if held is not None:
                use(*held)
            held = (i, k)
        use(*held)
        for j in range(leaves):
            sj = slice(j * LEAF, (j + 1) * LEAF)
            if len(rest) > 1:
                add(j, rest[0][:, sj])
            near_ref[:, sj] = jnp.zeros((cols, LEAF), F32) if acc[j] is None else acc[j]

    def near_part(rows, emb, x_tree, hn, *near):
        return call(
            lambda *refs: near_kernel(rows, *refs),
            jax.ShapeDtypeStruct((cols, points), F32),
            mult,
            emb,
            x_tree,
            hn,
            *near,
            flops=60 * 2 * 256**3,
            nbytes=6 << 20,
            name="near%d" % rows[0],
        )

    def low_edge(mult_ref, emb_ref, hn_ref, src_ref, near_in, near_ref):
        acc = [jnp.zeros((cols, LEAF), F32)] * W
        for q in range(W):
            sq, sp = slice(q * LEAF, (q + 1) * LEAF), slice(0, (q + 1) * LEAF)
            es = src_ref[0:width, sq]
            g = dot(jnp.transpose(es), emb_ref[:, sp])
            k = jnp.exp(g - (col_of(half_norm_row(es)) + hn_ref[:, sp])).astype(BF16)
            y = dot(src_ref[width:, sq], k)
            for t in range(q + 1):
                acc[t] = acc[t] + times(mult_ref, t, q - t, y[:, t * LEAF : (t + 1) * LEAF])
        near_ref[:, 0:halo] = near_in[:, 0:halo] + jnp.concatenate(acc, axis=1)
        near_ref[:, halo:] = near_in[:, halo:]

    def high_edge(mult_ref, emb_ref, hn_ref, src_ref, near_in, near_ref):
        acc = [jnp.zeros((cols, LEAF), F32)] * W
        for q in range(W):
            sq, sp = slice(q * LEAF, (q + 1) * LEAF), slice((leaves - W + q) * LEAF, points)
            es = src_ref[0:width, sq]
            g = dot(jnp.transpose(es), emb_ref[:, sp])
            k = jnp.exp(g - (col_of(half_norm_row(es)) + hn_ref[:, sp])).astype(BF16)
            y = dot(src_ref[width:, sq], k)
            for i in range(W - q):
                t = leaves - W + q + i
                acc[q + i] = acc[q + i] + (
                    times(mult_ref, t, leaves + q - t + W, y[:, i * LEAF : (i + 1) * LEAF])
                )
        near_ref[:, 0:last] = near_in[:, 0:last]
        near_ref[:, last:] = near_in[:, last:] + jnp.concatenate(acc, axis=1)

    def core_kernel(mult_ref, emb_ref, hn_ref, src_ref, near_in, near_ref):
        odd = jnp.bitwise_and(lax.axis_index("leaf"), 1)
        for code, edge in ((1, low_edge), (0, high_edge)):

            @pl.when(odd == code)
            def _():
                edge(mult_ref, emb_ref, hn_ref, src_ref, near_in, near_ref)

    def core_part(emb, hn, recv_a, near):
        return call(
            core_kernel,
            jax.ShapeDtypeStruct((cols, points), F32),
            mult,
            emb,
            hn,
            recv_a,
            near,
            flops=30 * 2 * 256**3,
            nbytes=3 << 20,
            name="edge_core",
        )

    def kernel_of(es, emb_ref, hn_ref, sp):
        g = dot(jnp.transpose(es), emb_ref[:, sp])
        return jnp.exp(g - (col_of(half_norm_row(es)) + hn_ref[:, sp])).astype(BF16)

    def told(src_ref, row, value):
        at = width + cols + row
        count = src_ref[at : at + 1, 0:LANES].astype(F32)
        return value * jnp.concatenate([count] * (LEAF // LANES), axis=1)

    def leaf(q):
        return slice(q * LEAF, (q + 1) * LEAF)

    def upper(mult_ref, emb_ref, hn_ref, x_ref, src_ref, near_ref, back_ref):
        k3 = kernel_of(src_ref[0:width, leaf(1)], emb_ref, hn_ref, slice(LEAF, 3 * LEAF))
        k2 = kernel_of(src_ref[0:width, leaf(0)], emb_ref, hn_ref, leaf(1))
        y3 = dot(src_ref[width : width + cols, leaf(1)], k3)
        y2 = dot(src_ref[width : width + cols, leaf(0)], k2)
        near_ref[:, leaf(1)] += times(mult_ref, 1, 1, y3[:, leaf(0)]) + times(mult_ref, 1, 0, y2)
        near_ref[:, leaf(2)] += times(mult_ref, 2, 0, y3[:, leaf(1)])
        back_ref[:, leaf(0)] = told(src_ref, 2, dot_nt(x_ref[:, leaf(1)], k2))
        back_ref[:, leaf(1)] = told(src_ref, 0, dot_nt(x_ref[:, leaf(1)], k3[:, leaf(0)])) + told(
            src_ref, 1, dot_nt(x_ref[:, leaf(2)], k3[:, leaf(1)])
        )

    def lower(mult_ref, emb_ref, hn_ref, x_ref, src_ref, near_ref, back_ref):
        k = kernel_of(src_ref[0:width, leaf(0)], emb_ref, hn_ref, slice(last, points))
        y = dot(src_ref[width : width + cols, leaf(0)], k)
        back = jnp.zeros((cols, LEAF), F32)
        for q in range(W):
            t = leaves - W + q
            near_ref[:, leaf(t)] += times(mult_ref, t, 2 * W - q, y[:, leaf(q)])
            back = back + told(src_ref, W - 1 - q, dot_nt(x_ref[:, leaf(t)], k[:, leaf(q)]))
        back_ref[:, leaf(0)] = back
        back_ref[:, leaf(1)] = jnp.zeros((cols, LEAF), F32)

    def chip_kernel(mult_ref, emb_ref, hn_ref, x_ref, one_ref, two_ref, near_in, near_ref, back_ref):
        near_ref[...] = near_in[...]
        turn = jnp.bitwise_and(lax.axis_index("leaf"), 3)
        for code, side, src_ref in (
            (1, lower, one_ref),
            (2, upper, one_ref),
            (3, lower, two_ref),
            (0, upper, two_ref),
        ):

            @pl.when(turn == code)
            def _():
                side(mult_ref, emb_ref, hn_ref, x_ref, src_ref, near_ref, back_ref)

    def chip_part(emb, recv_b1, recv_b2, near):
        return call(
            chip_kernel,
            [
                jax.ShapeDtypeStruct((cols, points), F32),
                jax.ShapeDtypeStruct((cols, UP * LEAF), F32),
            ],
            mult,
            emb,
            hn,
            x_tree,
            recv_b1,
            recv_b2,
            near,
            name="edge_chip",
        )

    table = []
    for lev, off, row in sorted(plan.entries, key=lambda e: e[2]):
        for i in range(plan.slots[lev]):
            side = (off >> plan.shift[lev]) & 1
            table.append(
                (
                    off,
                    (side * LEVELS + lev) * R + i,
                    (1 << plan.shift[lev]) - 1,
                    plan.slots[lev],
                )
            )
    table = jnp.array(table, jnp.int32).T
    own_w = LEVELS * R
    dest = table[1] + jnp.bitwise_and(pos ^ table[0], table[2]) * table[3]
    dest = dest[None, :]

    def join(*blocks):
        rows = sum(used for _, used in blocks)
        whole = all(used % 8 == 0 for _, used in blocks)
        pad = -rows % 8

        def join_kernel(*refs):
            if whole:
                row = 0
                for ref, (_, used) in zip(refs, blocks):
                    refs[-1][row : row + used, :] = ref[0:used, :]
                    row += used
            else:
                values = [ref[...].astype(F32)[0:used] for ref, (_, used) in zip(refs, blocks)]
                if pad:
                    values.append(jnp.zeros((pad, width), F32))
                refs[-1][...] = jnp.concatenate(values, axis=0).astype(BF16)

        return call(
            join_kernel,
            jax.ShapeDtypeStruct((rows + pad, width), BF16),
            *[v for v, _ in blocks],
            name="join",
        )

    after = lax.optimization_barrier
    block, used = owned[0], plan.slots[0]
    for bit in reversed(range(plan.bits)):
        level = plan.bits - bit
        stage = level - 1
        partner = lax.ppermute(block, "leaf", [(i, i ^ (1 << bit)) for i in range(n)])
        if stage == 0:
            partner, x_tree, dest = after((partner, x_tree, dest))
        if stage == 1:
            recv_a = lax.ppermute(cut_core(emb, x_tree), "leaf", pairs_a)
            near = near_part((0, 1), emb, x_tree, hn)
            partner, near = after((partner, near))
        if stage == 2:
            near = near_part((2, 3), emb, x_tree, hn, near)
            partner, near, recv_a = after((partner, near, recv_a))
        if stage == 3:
            near = near_part(tuple(range(4, leaves)), emb, x_tree, hn, near)
            recv_b2 = lax.ppermute(cut_chip(emb, x_tree), "leaf", pairs(3))
            near = core_part(emb, hn, recv_a, near)
            partner, near = after((partner, near))
        if bit:
            more = [(owned[level], plan.slots[level])] if level < LEVELS else []
            block = join((block, used), (partner, used), *more)
            used = 2 * used + sum(slots for _, slots in more)
            block, x_tree, emb = after((block, x_tree, emb))
    half = plan.size // 2

    def sorted_rows(first, dest_ref, *refs):
        at = lax.broadcasted_iota(jnp.int32, (own_w, half), 0)
        total = None
        for i, ref in enumerate(refs):
            d = dest_ref[:, i * half : (i + 1) * half] - first
            term = dot(jnp.where(at == d, 1.0, 0.0).astype(BF16), ref[...])
            total = term if total is None else total + term
        return total.astype(BF16)

    def own_kernel(block_ref, other_ref, dest_ref, emb_ref, x_ref, hn_ref, z_ref):
        sk = sorted_rows(0, dest_ref, block_ref, other_ref)
        hs = half_norm_col(sk)
        z = jnp.zeros((cols, own_w), F32)
        held = None
        for c in range(0, leaves, 2):
            sl = slice(c * LEAF, (c + 2) * LEAF)
            k = jnp.exp(dot(sk, emb_ref[:, sl]) - (hs + hn_ref[:, sl])).astype(BF16)
            if held is not None:
                z = z + dot_nt(x_ref[:, held[0]], held[1])
            held = (sl, k)
        z_ref[...] = z + dot_nt(x_ref[:, held[0]], held[1])

    z = call(
        own_kernel,
        jax.ShapeDtypeStruct((cols, own_w), F32),
        block,
        partner,
        dest,
        emb,
        x_tree,
        hn,
        flops=50 * 2 * 256**3,
        nbytes=4 << 20,
        name="own",
        cost=3_000_000_000,
    )

    def far_kernel(block_ref, other_ref, dest_ref, emb_ref, hn_ref, out_ref):
        sk = sorted_rows(own_w, dest_ref, block_ref, other_ref)
        hs = half_norm_col(sk)
        for c in range(0, leaves, 2):
            sl = slice(c * LEAF, (c + 2) * LEAF)
            g = dot(sk, emb_ref[:, sl])
            out_ref[:, sl] = jnp.exp(g - (hs + hn_ref[:, sl])).astype(BF16)

    def far_part(block, partner, emb, hn):
        return call(
            far_kernel,
            jax.ShapeDtypeStruct((own_w, points), BF16),
            block,
            partner,
            dest,
            emb,
            hn,
            flops=30 * 2 * 256**3,
            nbytes=4 << 20,
            name="far",
        )

    level_of = lax.broadcasted_iota(jnp.int32, (1, own_w), 1) // R
    for stage, bit in enumerate([0] + list(range(3, plan.bits)) + [2, 1]):
        heard = lax.ppermute(z, "leaf", [(i, i ^ (1 << bit)) for i in range(n)])
        if stage == 0:
            far_k = far_part(block, partner, emb, hn)
            heard, far_k, recv_b2 = after((heard, far_k, recv_b2))
        if stage == 0:
            recv_b1 = lax.ppermute(cut_chip(emb, x_tree), "leaf", pairs(1))
        if stage == 3:
            near, back = chip_part(emb, recv_b1, recv_b2, near)
            heard, near, back = after((heard, near, back))
        if stage == 4:
            back = lax.ppermute(back, "leaf", pairs(1, 3))
        swap = level_of == plan.bits - 1 - bit
        add = level_of < plan.bits - 1 - bit
        z = jnp.where(add, z + heard, jnp.where(swap, heard, z))
        z, emb = after((z, emb))

    def last_kernel(z_ref, core_ref, far_ref, back_ref, inv_ref, near_ref, out_ref):
        me = lax.axis_index("leaf")
        weights = []
        for l in range(LEVELS):
            node = 2 ** (l + 1) - 2 + (jnp.right_shift(me, plan.shift[l]) ^ 1)
            weights.append(
                jnp.dot(
                    z_ref[:, l * R : (l + 1) * R],
                    core_ref[node],
                    precision=lax.Precision.HIGHEST,
                    preferred_element_type=F32,
                ).astype(BF16)
            )
        w = jnp.concatenate(weights, axis=1)
        tree = near_ref[...] + dot(w, far_ref[...])
        even = jnp.bitwise_and(me, 1) == 0
        low_back = jnp.where(even, back_ref[:, 0:LEAF], 0.0)
        high_back = jnp.where(even, 0.0, back_ref[...])
        tree = tree + jnp.concatenate(
            [low_back, jnp.zeros((cols, points - (1 + UP) * LEAF), F32), high_back], axis=1
        )
        top = tree.astype(BF16)
        rest = (tree - top.astype(F32)).astype(BF16)
        stack = jnp.concatenate(
            [
                jnp.concatenate([v[:, h * LANES : (h + 1) * LANES] for v in (top, rest)], axis=1)
                for h in range(groups)
            ],
            axis=0,
        )
        low = jnp.bitwise_and(inv_ref[...], LANES - 1)
        high = jnp.right_shift(inv_ref[...], LANES.bit_length() - 1)
        hot = jnp.where(
            lax.broadcasted_iota(jnp.int32, (LANES, points), 0) == low, 1.0, 0.0
        ).astype(BF16)
        for c in range(leaves):
            sl = slice(c * LEAF, (c + 1) * LEAF)
            y = dot(stack, jnp.concatenate([hot[:, sl]] * 2, axis=0))
            out = jnp.zeros((cols, LEAF), F32)
            for h in range(groups):
                out = jnp.where(high[:, sl] == h, y[h * cols : (h + 1) * cols], out)
            out_ref[:, sl] = out

    return call(
        last_kernel,
        jax.ShapeDtypeStruct((cols, points), F32),
        z,
        core,
        far_k,
        back,
        inv,
        near,
        flops=30 * 2 * 256**3,
        nbytes=2 << 20,
        name="last",
    )


def solution(mesh):
    return jax.shard_map(
        body,
        mesh=mesh,
        in_specs=(
            P(None, ("groups", "leaf")),
            P(None, ("groups", "leaf")),
            P(("groups", "leaf"), None),
            P(("groups", "leaf"), None),
            P(("groups", "leaf"), None),
            P("groups", None),
            P("groups", None, None),
        ),
        out_specs=P(None, ("groups", "leaf")),
        check_vma=False,
    )
```
